32 devices in a mesh: grow: 8 (over z, y), lat: 4 (over x, core).
Axes of the slice: x: 2, y: 2, z: 4, core: 2. Of those that a mesh axis runs over, the one named last changes fastest.
Arguments:
- labels: int32 [128, 128, 128], P('grow', 'lat'), may hold values from 0 to 3
- roughness: float32 [4, 128, 128, 128], P(None, 'grow', 'lat'), may hold values from 0.1 to 1
- potential: float32 [2, 128, 128, 128], P(None, 'grow', 'lat'), may hold values from -3 to 3
- grad_coef: float32 [4, 3], replicated, may hold values from 0.2 to 1
- composition: float32 [4, 2], replicated, may hold values from -2 to 2
- latent: float32 [4], replicated, may hold values from 0.5 to 2
- diffusivity: float32 [2], replicated, may hold values from 0.5 to 2
- melt_table: float32 [16, 2], replicated, may hold values from -1 to 1
- melt_index: int32 [4, 8, 128, 128], P(None, None, 'lat'), may hold values from 0 to 15
Outputs:
- phases: float32 [4, 128, 128, 128], P(None, 'grow', 'lat')
- potentials: float32 [2, 128, 128, 128], P(None, 'grow', 'lat')
The draws below stay inside these ranges and needn't reach their ends.
All inputs are finite; a program needn't handle non-finite values.
Results may differ from the reference program's by a relative error of at most 0.00025.
Values sent between devices are 32-bit elements; how exact they have to be, the bound alone decides.
No kernel may reach another device: no remote copies, remote signals or barrier semaphores. Data moves between devices by JAX's collectives and lax.ppermute only.
A program may use at most 64 MiB of HBM per device.

```python
import math
import jax
import jax.numpy as jnp

NY = 128
STEPS = 4
ROUNDS = 4
SHIFT = 8
MELT = 16
NG = 128
NX = 128


def plant(entries, key, low, largest):
    index_at = [jax.random.randint(jax.random.fold_in(key, axis), (), 0, length) for axis, length in enumerate(entries.shape)]
    longest = entries.shape.index(max(entries.shape))
    beside = index_at[:longest] + [(index_at[longest] + 1) % entries.shape[longest]] + index_at[longest + 1:]
    return entries.at[tuple(index_at)].set(low).at[tuple(beside)].set(largest)


def level_of(own_key, dims, pieces, low, high):
    def one(axis_at, shards_of):
        draws = jax.random.uniform(jax.random.fold_in(jax.random.fold_in(own_key, 6), axis_at), (shards_of,), jnp.float32, low / len(pieces), high / len(pieces))
        return jnp.repeat(jnp.exp(draws), dims[axis_at] // shards_of).reshape((-1,) + (1,) * (len(dims) - axis_at - 1))

    gain = one(*pieces[0])
    for cut in pieces[1:]:
        gain = gain * one(*cut)
    return gain


def bell_draw(own_key, shape, spread, most, pieces=(), kind=jnp.bfloat16):
    array = spread * jax.random.normal(own_key, shape, jnp.float32)
    if pieces:
        array = array * level_of(own_key, shape, pieces, -0.22, 0.18)
    return jnp.clip(array, -most, most).astype(kind)


def setup_inputs(seed: int = 0) -> dict:
    splits = jax.random.split(jax.random.key(seed), 10)
    labels = plant(jax.random.randint(splits[0], (NG, NX, NY), 0, 4), jax.random.fold_in(splits[0], 1), 0, 3).astype(jnp.int32)
    roughness = jnp.clip(jnp.exp(math.log(1.0) - 2.3025851 * jax.random.uniform(splits[1], (4, NG, NX, NY), jnp.float32) ** level_of(splits[1], (4, NG, NX, NY), ((1, 8), (2, 4)), -0.2, 0.2)), 0.1, 1.0)
    potential = bell_draw(splits[2], (2, NG, NX, NY), 0.5, 3.0, ((1, 8), (2, 4)), jnp.float32)
    grad_coef = jnp.clip(jnp.exp(jax.random.uniform(splits[3], (4, 3), jnp.float32, math.log(0.2), math.log(1.0))), 0.2, 1.0)
    composition = bell_draw(splits[4], (4, 2), 0.5, 2.0, (), jnp.float32)
    latent = jnp.clip(jax.random.uniform(splits[5], (4,), jnp.float32, 0.5, 2.0), 0.5, 2.0)
    diffusivity = jnp.clip(jnp.exp(jax.random.uniform(splits[6], (2,), jnp.float32, math.log(0.5), math.log(2.0))), 0.5, 2.0)
    melt_table = jnp.clip(jax.random.uniform(splits[7], (MELT, 2), jnp.float32, -1.0, 1.0), -1.0, 1.0)
    melt_index = plant(jax.random.randint(splits[8], (ROUNDS, SHIFT, NX, NY), 0, MELT), jax.random.fold_in(splits[8], 1), 0, MELT - 1).astype(jnp.int32)
    return {"labels": labels, "roughness": roughness, "potential": potential, "grad_coef": grad_coef, "composition": composition, "latent": latent, "diffusivity": diffusivity, "melt_table": melt_table, "melt_index": melt_index}


def advance(padded, grad_coef, composition, latent, diffusivity, first, total):
    center = padded[:, 1:-1, 1:-1]
    gsum = padded[:, 2:, 1:-1] + padded[:, :-2, 1:-1] - 2.0 * center
    xsum = padded[:, 1:-1, 2:] + padded[:, 1:-1, :-2] - 2.0 * center
    ysum = jnp.roll(center, 1, 3) + jnp.roll(center, -1, 3) - 2.0 * center
    fracs = center[:4]
    chem = center[4:]
    lap_phi = (grad_coef[:, 0][:, None, None, None] * gsum[:4]
               + grad_coef[:, 1][:, None, None, None] * xsum[:4]
               + grad_coef[:, 2][:, None, None, None] * ysum[:4])
    lap_mu = gsum[4:] + xsum[4:] + ysum[4:]
    rows = center.shape[1]
    theta = ((jnp.arange(rows, dtype=jnp.int32) + first).astype(jnp.float32) - 0.5 * total) / total
    psi = (composition[:, 0][:, None, None, None] * chem[0]
           + composition[:, 1][:, None, None, None] * chem[1]
           + latent[:, None, None, None] * theta[None, :, None, None])
    summed = jnp.sum(fracs, axis=0)
    rhs = lap_phi - 1.0 * (summed[None] - fracs) - psi
    rhs = rhs - jnp.mean(rhs, axis=0)[None]
    trial = fracs + 0.04 * rhs
    clipped = jnp.clip(trial, 0.0, 1.0)
    newphi = clipped / jnp.sum(clipped, axis=0)[None]
    change = newphi - fracs
    release = jnp.stack([jnp.sum(composition[:, 0][:, None, None, None] * change, axis=0),
                         jnp.sum(composition[:, 1][:, None, None, None] * change, axis=0)])
    newmu = chem + 0.04 * diffusivity[:, None, None, None] * lap_mu - release
    return jnp.concatenate([newphi, newmu], axis=0)


def reference(labels, roughness, potential, grad_coef, composition, latent, diffusivity, melt_table, melt_index):
    ngrid = labels.shape[0]
    kinds = jnp.arange(4, dtype=jnp.int32)[:, None, None, None]
    onehot = (labels[None] == kinds).astype(jnp.float32)
    fracs = (3.0 * onehot + roughness) / (3.0 + jnp.sum(roughness, axis=0))[None]
    state = jnp.concatenate([fracs, potential], axis=0)
    total = float(ngrid)
    for turn in range(ROUNDS):
        for step in range(STEPS):
            padded = jnp.pad(state, ((0, 0), (1, 1), (0, 0), (0, 0)), mode="edge")
            padded = jnp.concatenate([padded[:, :, -1:], padded, padded[:, :, :1]], axis=2)
            state = advance(padded, grad_coef, composition, latent, diffusivity, SHIFT * turn, total)
        chosen = melt_index[turn]
        melt_mu = jnp.moveaxis(melt_table[chosen], -1, 0)
        zeros = jnp.zeros(chosen.shape, jnp.float32)
        fresh = jnp.concatenate([jnp.stack([zeros, zeros, zeros, zeros + 1.0]), melt_mu], axis=0)
        state = jnp.concatenate([state[:, SHIFT:], fresh], axis=1)
    return state[:4], state[4:]
```

```python
import functools

import jax
import jax.numpy as jnp
from jax import lax
from jax.experimental import pallas as pl
from jax.experimental.pallas import tpu as pltpu
from jax.sharding import PartitionSpec as P

STEPS = 4
ROUNDS = 4
SHIFT = 8
JUMPS = (12, 8, 4, 8)
SENT = 5
PAD = 8
DT = 0.04
AXES = ("grow", "lat")
GRAD, CENTER, COUPLE, LATENT, RELEASE, SPREAD, STAY, MELT = 0, 12, 16, 24, 28, 36, 38, 40


def scalar_table(grad_coef, composition, latent, diffusivity, melt_table):
    scaled = DT * grad_coef
    return jnp.concatenate(
        [
            scaled.reshape(-1),
            1.0 + DT - 2.0 * jnp.sum(scaled, axis=1),
            (DT * composition).reshape(-1),
            DT * latent,
            composition.reshape(-1),
            DT * diffusivity,
            1.0 - 6.0 * DT * diffusivity,
            melt_table.reshape(-1),
        ]
    )


def round_kernel(
    turn, place_of, base, keeps, last, sizes, table, own, above, left, right, index, *rest
):
    outs, (even, odd) = rest[:-2], rest[-2:]
    ng, block, rows = sizes
    kept, total = own.shape[1], float(ng * block)
    height = block + 2 * STEPS
    place = place_of()
    start = place * block + base - STEPS
    lowest = SHIFT * turn - start
    top = ng * block + SHIFT * turn - 1 - start

    def fill(source, e_from, e_to):
        fields = [source[f, e_from] for f in range(SENT)]
        for f, value in zip((0, 1, 2, 4, 5), fields):
            even[f, e_to, PAD : PAD + rows] = value
        even[3, e_to, PAD : PAD + rows] = 1.0 - fields[0] - fields[1] - fields[2]
        for side, at in ((left, PAD - STEPS), (right, PAD + rows)):
            fields = [side[f, e_to] for f in range(SENT)]
            for f, value in zip((0, 1, 2, 4, 5), fields):
                even[f, e_to, at : at + STEPS] = value
            even[3, e_to, at : at + STEPS] = 1.0 - fields[0] - fields[1] - fields[2]

    @pl.loop(0, kept)
    def _(e):
        fill(own, e, e)

    @pl.loop(0, height - kept)
    def _(e):
        fill(above, e, e + kept)

    def advance(src, e, at):
        window = pl.ds(at, 8)
        up, down = jnp.minimum(e + 1, top), jnp.maximum(e - 1, lowest)
        theta = ((e + start).astype(jnp.float32) - 0.5 * total) / total
        mid = [src[f, e, window] for f in range(6)]
        gsum = [src[f, up, window] + src[f, down, window] for f in range(6)]
        xsum = [src[f, e, pl.ds(at + 1, 8)] + src[f, e, pl.ds(at - 1, 8)] for f in range(6)]
        ysum = [pltpu.roll(v, 1, 1) + pltpu.roll(v, v.shape[1] - 1, 1) for v in mid]
        m0, m1 = mid[4], mid[5]
        guess = []
        for a in range(4):
            guess.append(
                table[GRAD + 3 * a] * gsum[a]
                + table[GRAD + 3 * a + 1] * xsum[a]
                + table[GRAD + 3 * a + 2] * ysum[a]
                + table[CENTER + a] * mid[a]
                - table[COUPLE + 2 * a] * m0
                - table[COUPLE + 2 * a + 1] * m1
                - table[LATENT + a] * theta
            )
        phase_sum = mid[0] + mid[1] + mid[2] + mid[3]
        mean = 0.25 * (guess[0] + guess[1] + guess[2] + guess[3] - phase_sum)
        clipped = [jnp.clip(g - mean, 0.0, 1.0) for g in guess]
        inverse = 1.0 / (clipped[0] + clipped[1] + clipped[2] + clipped[3])
        new = [c * inverse for c in clipped]
        change = [n - v for n, v in zip(new, mid)]
        for k in range(2):
            release = table[RELEASE + k] * change[0]
            for a in range(1, 4):
                release = release + table[RELEASE + 2 * a + k] * change[a]
            sides = gsum[4 + k] + xsum[4 + k] + ysum[4 + k]
            new.append(table[SPREAD + k] * sides + table[STAY + k] * mid[4 + k] - release)
        return new

    buffers = (even, odd)
    for step in range(1, STEPS):
        src, dst = buffers[(step - 1) % 2], buffers[step % 2]

        @pl.loop(step, height - step)
        def _(e, src=src, dst=dst):
            for t in range(rows // 8 + 1):
                at = PAD - STEPS + 8 * t
                for f, value in enumerate(advance(src, e, at)):
                    dst[f, e, pl.ds(at, 8)] = value

    src = buffers[(STEPS - 1) % 2]
    if last:
        phases, potentials = outs

        def put(o, here, new):
            for a in range(4):
                phases[a, o, here] = new[a]
            for k in range(2):
                potentials[k, o, here] = new[4 + k]

    else:
        climbing, staying = outs

        def put(o, here, new):
            sent = [new[f] for f in (0, 1, 2, 4, 5)]

            @pl.when(o < climbing.shape[1])
            def _():
                for f in range(SENT):
                    climbing[f, o, here] = sent[f]

            @pl.when(o >= keeps)
            def _():
                for f in range(SENT):
                    staying[f, o - keeps, here] = sent[f]

    @pl.loop(0, block)
    def _(o):
        for t in range(rows // 8):
            put(o, pl.ds(8 * t, 8), advance(src, o + STEPS, PAD + 8 * t))

    fresh = ng * block + SHIFT * turn - (ng - 1) * block - base

    @pl.when(place == ng - 1)
    def _():
        @pl.loop(0, SHIFT)
        def _(j):
            for t in range(rows // 8):
                here = pl.ds(8 * t, 8)
                row = index[j, here]
                mu = [jnp.zeros(row.shape, jnp.float32)] * 2
                for m in range((table.shape[0] - MELT) // 2):
                    mu = [jnp.where(row == m, table[MELT + 2 * m + k], mu[k]) for k in range(2)]
                none = jnp.zeros(row.shape, jnp.float32)
                put(fresh + j, here, [none, none, none, none + 1.0] + mu)


def prepare_kernel(labels, roughness, potential, climbing, staying):
    skipped = labels.shape[0] - staying.shape[1]

    @pl.loop(0, labels.shape[0])
    def _(o):
        kind = labels[o]
        rough = [roughness[a, o] for a in range(4)]
        inverse = 1.0 / (3.0 + rough[0] + rough[1] + rough[2] + rough[3])
        new = [(jnp.where(kind == a, 3.0, 0.0) + rough[a]) * inverse for a in range(3)]
        new += [potential[0, o], potential[1, o]]
        for f in range(SENT):
            climbing[f, o] = new[f]

        @pl.when(o >= skipped)
        def _():
            for f in range(SENT):
                staying[f, o - skipped] = new[f]


def on_device(ng, nl, labels, roughness, potential, grad_coef, composition, latent, diffusivity, melt_table, melt_index):
    block, rows, lanes = labels.shape
    height = block + 2 * STEPS
    vmem = pl.BlockSpec(memory_space=pltpu.VMEM)
    smem = pl.BlockSpec(memory_space=pltpu.SMEM)
    f32 = jnp.float32
    table = scalar_table(grad_coef, composition, latent, diffusivity, melt_table)

    def home(g, l):
        return g * nl + l

    def away(g, l):
        return (g // 2 * 2 + (l % 2 ^ (l // 2 % 2))) * nl + l // 2 * 2 + g % 2

    def home_place():
        return lax.axis_index("grow")

    def away_place():
        return lax.axis_index("grow") // 2 * 2 + lax.axis_index("lat") % 2

    blocks = [(g, l) for g in range(ng) for l in range(nl)]

    def moved(array, before, after, climb):
        route = [(before(g + climb, l), after(g, l)) for g, l in blocks if g + climb < ng]
        return lax.ppermute(array, AXES, route)

    def sides(own, above, where):
        first = jnp.concatenate([own[:, :, :STEPS], above[:, :, :STEPS]], axis=1)
        final = jnp.concatenate([own[:, :, rows - STEPS :], above[:, :, rows - STEPS :]], axis=1)
        left = lax.ppermute(final, AXES, [(where(g, l), where(g, (l + 1) % nl)) for g, l in blocks])
        right = lax.ppermute(first, AXES, [(where(g, (l + 1) % nl), where(g, l)) for g, l in blocks])
        return left, right

    def sizes_of(jump):
        return jump + STEPS, block - jump + STEPS

    def piece(planes):
        return jax.ShapeDtypeStruct((SENT, planes, rows, lanes), f32)

    climbing, staying = pl.pallas_call(
        prepare_kernel,
        out_shape=[piece(n) for n in sizes_of(JUMPS[0])],
        in_specs=[vmem] * 3,
        out_specs=[vmem] * 2,
        name="prepare",
    )(labels, roughness, potential)

    away_index = lax.ppermute(
        melt_index[: ROUNDS - 1],
        AXES,
        [(home(ng - 1, l), away(ng - 1, l)) for l in range(nl)],
    )

    base = 0
    for turn in range(ROUNDS):
        before = home if turn == 0 else away
        after = home if turn == ROUNDS - 1 else away
        above = moved(climbing, before, after, 1)
        own = staying if before is after else moved(staying, before, after, 0)
        left, right = sides(own, above, after)
        base += JUMPS[turn]
        last = turn == ROUNDS - 1
        if last:
            shapes = [jax.ShapeDtypeStruct((n, block, rows, lanes), f32) for n in (4, 2)]
            keeps = 0
        else:
            shapes = [piece(n) for n in sizes_of(JUMPS[turn + 1])]
            keeps = block - shapes[1].shape[1]
        outs = pl.pallas_call(
            functools.partial(
                round_kernel,
                turn,
                home_place if last else away_place,
                base,
                keeps,
                last,
                (ng, block, rows),
            ),
            out_shape=shapes,
            in_specs=[smem] + [vmem] * 5,
            out_specs=[vmem] * 2,
            scratch_shapes=[pltpu.VMEM((6, height, rows + 2 * PAD, lanes), f32)] * 2,
            compiler_params=pltpu.CompilerParams(vmem_limit_bytes=40 << 20),
            name="advance",
        )(table, own, above, left, right, melt_index[turn] if last else away_index[turn])
        climbing, staying = outs
    return outs[0], outs[1]


def solution(mesh):
    ng, nl = mesh.shape["grow"], mesh.shape["lat"]
    placed = (
        P("grow", "lat", None),
        P(None, "grow", "lat", None),
        P(None, "grow", "lat", None),
        P(),
        P(),
        P(),
        P(),
        P(),
        P(None, None, "lat", None),
    )
    return jax.shard_map(
        functools.partial(on_device, ng, nl),
        mesh=mesh,
        in_specs=placed,
        out_specs=(P(None, "grow", "lat", None), P(None, "grow", "lat", None)),
        check_vma=False,
    )
```

```python
import functools

import jax
import jax.numpy as jnp
from jax import lax
from jax.experimental import pallas as pl
from jax.experimental.pallas import tpu as pltpu
from jax.sharding import PartitionSpec as P

STEPS = 4
ROUNDS = 4
SHIFT = 8
JUMPS = (12, 8, 4, 8)
SENT = 5
PAD = 8
DT = 0.04
PLANES = 2
AXES = ("grow", "lat")
GRAD, CENTER, COUPLE, LATENT, RELEASE, SPREAD, STAY, MELT = 0, 12, 16, 24, 28, 36, 38, 40


def scalar_table(grad_coef, composition, latent, diffusivity, melt_table):
    scaled = DT * grad_coef
    return jnp.concatenate(
        [
            scaled.reshape(-1),
            1.0 + DT - 2.0 * jnp.sum(scaled, axis=1),
            (DT * (composition - jnp.mean(composition, axis=0))).reshape(-1),
            DT * (latent - jnp.mean(latent)),
            (composition - composition[3]).reshape(-1),
            DT * diffusivity,
            1.0 - 6.0 * DT * diffusivity,
            melt_table.reshape(-1),
        ]
    )


def round_kernel(
    turn, place_of, base, keeps, last, sizes, table, own, above, left, right, index, *rest
):
    outs, (even, odd) = rest[:-2], rest[-2:]
    ng, block, rows = sizes
    kept, total = own.shape[1], float(ng * block)
    height = block + 2 * STEPS
    place = place_of()
    start = place * block + base - STEPS
    lowest = SHIFT * turn - start
    top = ng * block + SHIFT * turn - 1 - start

    def fill(source, e_from, e_to):
        fields = [source[f, e_from] for f in range(SENT)]
        for f, value in zip((0, 1, 2, 4, 5), fields):
            even[f, e_to, PAD : PAD + rows] = value
        even[3, e_to, PAD : PAD + rows] = 1.0 - fields[0] - fields[1] - fields[2]
        for side, at in ((left, PAD - STEPS), (right, PAD + rows)):
            fields = [side[f, e_to] for f in range(SENT)]
            for f, value in zip((0, 1, 2, 4, 5), fields):
                even[f, e_to, at : at + STEPS] = value
            even[3, e_to, at : at + STEPS] = 1.0 - fields[0] - fields[1] - fields[2]

    @pl.loop(0, kept)
    def _(e):
        fill(own, e, e)

    @pl.loop(0, height - kept)
    def _(e):
        fill(above, e, e + kept)

    def advance(src, e, at):
        window = pl.ds(at, 8)
        up, down = jnp.minimum(e + 1, top), jnp.maximum(e - 1, lowest)
        theta = ((e + start).astype(jnp.float32) - 0.5 * total) / total
        mid = [src[f, e, window] for f in range(6)]
        gsum = [src[f, up, window] + src[f, down, window] for f in range(6)]
        xsum = [src[f, e, pl.ds(at + 1, 8)] + src[f, e, pl.ds(at - 1, 8)] for f in range(6)]
        ysum = [pltpu.roll(v, 1, 1) + pltpu.roll(v, v.shape[1] - 1, 1) for v in mid]
        m0, m1 = mid[4], mid[5]
        spread = [
            table[GRAD + 3 * a] * gsum[a]
            + table[GRAD + 3 * a + 1] * xsum[a]
            + table[GRAD + 3 * a + 2] * ysum[a]
            + table[CENTER + a] * mid[a]
            for a in range(4)
        ]
        mean = 0.25 * (spread[0] + spread[1] + spread[2] + spread[3]) - 0.25
        trial = [
            spread[a]
            - mean
            - table[COUPLE + 2 * a] * m0
            - table[COUPLE + 2 * a + 1] * m1
            - table[LATENT + a] * theta
            for a in range(3)
        ]
        trial.append(1.0 - trial[0] - trial[1] - trial[2])
        clipped = [jnp.clip(t, 0.0, 1.0) for t in trial]
        inverse = 1.0 / (clipped[0] + clipped[1] + clipped[2] + clipped[3])
        new = [c * inverse for c in clipped]
        change = [n - v for n, v in zip(new[:3], mid[:3])]
        for k in range(2):
            release = table[RELEASE + k] * change[0]
            for a in range(1, 3):
                release = release + table[RELEASE + 2 * a + k] * change[a]
            sides = gsum[4 + k] + xsum[4 + k] + ysum[4 + k]
            new.append(table[SPREAD + k] * sides + table[STAY + k] * mid[4 + k] - release)
        return new

    def sweep(src, first, stop, tiles, put):
        @pl.loop(0, (stop - first) // PLANES)
        def _(i):
            for p in range(PLANES):
                e = first + PLANES * i + p
                for at in tiles:
                    put(e, at, advance(src, e, at))

    buffers = (even, odd)
    for step in range(1, STEPS):
        src, dst = buffers[(step - 1) % 2], buffers[step % 2]

        def keep(e, at, new, dst=dst):
            for f in range(6):
                dst[f, e, pl.ds(at, 8)] = new[f]

        sweep(src, step, height - step, [PAD - STEPS + 8 * t for t in range(rows // 8 + 1)], keep)

    src = buffers[(STEPS - 1) % 2]

    def put(climbs, stays):
        def write(e, at, new):
            o, here = e - STEPS, pl.ds(at - PAD, 8)
            if last:
                for a in range(4):
                    outs[0][a, o, here] = new[a]
                for k in range(2):
                    outs[1][k, o, here] = new[4 + k]
                return
            for f, value in enumerate([new[f] for f in (0, 1, 2, 4, 5)]):
                if climbs:
                    outs[0][f, o, here] = value
                if stays:
                    outs[1][f, o - keeps, here] = value

        return write

    climbed = block if last else outs[0].shape[1]
    for first, stop in ((0, keeps), (keeps, climbed), (climbed, block)):
        write = put(stop <= climbed, first >= keeps)
        sweep(src, first + STEPS, stop + STEPS, [PAD + 8 * t for t in range(rows // 8)], write)

    fresh = ng * block + SHIFT * turn - (ng - 1) * block - base

    @pl.when(place == ng - 1)
    def _():
        for j in range(SHIFT):
            write = put(fresh + j < climbed, fresh + j >= keeps)
            for t in range(rows // 8):
                row = index[j, pl.ds(8 * t, 8)]
                mu = [jnp.zeros(row.shape, jnp.float32)] * 2
                for m in range((table.shape[0] - MELT) // 2):
                    mu = [jnp.where(row == m, table[MELT + 2 * m + k], mu[k]) for k in range(2)]
                none = jnp.zeros(row.shape, jnp.float32)
                write(fresh + j + STEPS, PAD + 8 * t, [none, none, none, none + 1.0] + mu)


def prepare_kernel(labels, roughness, potential, climbing, staying):
    skipped = labels.shape[0] - staying.shape[1]

    @pl.loop(0, labels.shape[0])
    def _(o):
        kind = labels[o]
        rough = [roughness[a, o] for a in range(4)]
        inverse = 1.0 / (3.0 + rough[0] + rough[1] + rough[2] + rough[3])
        new = [(jnp.where(kind == a, 3.0, 0.0) + rough[a]) * inverse for a in range(3)]
        new += [potential[0, o], potential[1, o]]
        for f in range(SENT):
            climbing[f, o] = new[f]

        @pl.when(o >= skipped)
        def _():
            for f in range(SENT):
                staying[f, o - skipped] = new[f]


def on_device(ng, nl, labels, roughness, potential, grad_coef, composition, latent, diffusivity, melt_table, melt_index):
    block, rows, lanes = labels.shape
    height = block + 2 * STEPS
    vmem = pl.BlockSpec(memory_space=pltpu.VMEM)
    smem = pl.BlockSpec(memory_space=pltpu.SMEM)
    f32 = jnp.float32
    table = scalar_table(grad_coef, composition, latent, diffusivity, melt_table)

    def home(g, l):
        return g * nl + l

    def away(g, l):
        return (g // 2 * 2 + (l % 2 ^ (l // 2 % 2))) * nl + l // 2 * 2 + g % 2

    def home_place():
        return lax.axis_index("grow")

    def away_place():
        return lax.axis_index("grow") // 2 * 2 + lax.axis_index("lat") % 2

    blocks = [(g, l) for g in range(ng) for l in range(nl)]

    def moved(array, before, after, climb):
        route = [(before(g + climb, l), after(g, l)) for g, l in blocks if g + climb < ng]
        return lax.ppermute(array, AXES, route)

    def sides(own, above, where):
        first = jnp.concatenate([own[:, :, :STEPS], above[:, :, :STEPS]], axis=1)
        final = jnp.concatenate([own[:, :, rows - STEPS :], above[:, :, rows - STEPS :]], axis=1)
        left = lax.ppermute(final, AXES, [(where(g, l), where(g, (l + 1) % nl)) for g, l in blocks])
        right = lax.ppermute(first, AXES, [(where(g, (l + 1) % nl), where(g, l)) for g, l in blocks])
        return left, right

    def sizes_of(jump):
        return jump + STEPS, block - jump + STEPS

    def piece(planes):
        return jax.ShapeDtypeStruct((SENT, planes, rows, lanes), f32)

    climbing, staying = pl.pallas_call(
        prepare_kernel,
        out_shape=[piece(n) for n in sizes_of(JUMPS[0])],
        in_specs=[vmem] * 3,
        out_specs=[vmem] * 2,
        name="prepare",
    )(labels, roughness, potential)

    away_index = lax.ppermute(
        melt_index[: ROUNDS - 1],
        AXES,
        [(home(ng - 1, l), away(ng - 1, l)) for l in range(nl)],
    )

    base = 0
    for turn in range(ROUNDS):
        before = home if turn == 0 else away
        after = home if turn == ROUNDS - 1 else away
        above = moved(climbing, before, after, 1)
        own = staying if before is after else moved(staying, before, after, 0)
        left, right = sides(own, above, after)
        base += JUMPS[turn]
        last = turn == ROUNDS - 1
        if last:
            shapes = [jax.ShapeDtypeStruct((n, block, rows, lanes), f32) for n in (4, 2)]
            keeps = 0
        else:
            shapes = [piece(n) for n in sizes_of(JUMPS[turn + 1])]
            keeps = block - shapes[1].shape[1]
        outs = pl.pallas_call(
            functools.partial(
                round_kernel,
                turn,
                home_place if last else away_place,
                base,
                keeps,
                last,
                (ng, block, rows),
            ),
            out_shape=shapes,
            in_specs=[smem] + [vmem] * 5,
            out_specs=[vmem] * 2,
            scratch_shapes=[pltpu.VMEM((6, height, rows + 2 * PAD, lanes), f32)] * 2,
            compiler_params=pltpu.CompilerParams(vmem_limit_bytes=40 << 20),
            name="advance",
        )(table, own, above, left, right, melt_index[turn] if last else away_index[turn])
        climbing, staying = outs
    return outs[0], outs[1]


def solution(mesh):
    ng, nl = mesh.shape["grow"], mesh.shape["lat"]
    placed = (
        P("grow", "lat", None),
        P(None, "grow", "lat", None),
        P(None, "grow", "lat", None),
        P(),
        P(),
        P(),
        P(),
        P(),
        P(None, None, "lat", None),
    )
    return jax.shard_map(
        functools.partial(on_device, ng, nl),
        mesh=mesh,
        in_specs=placed,
        out_specs=(P(None, "grow", "lat", None), P(None, "grow", "lat", None)),
        check_vma=False,
    )
```

```python
import functools

import jax
import jax.numpy as jnp
from jax import lax
from jax.experimental import pallas as pl
from jax.experimental.pallas import tpu as pltpu
from jax.sharding import PartitionSpec as P

STEPS = 4
ROUNDS = 4
SHIFT = 8
SENT = (0, 1, 2, 4, 5)
PAD = 8
DT = 0.04
PLANES = 2
AXES = ("grow", "lat")
GRAD, CENTER, COUPLE, LATENT, RELEASE, SPREAD, STAY, MELT = 0, 12, 16, 24, 28, 36, 38, 40


def scalar_table(grad_coef, composition, latent, diffusivity, melt_table):
    scaled = DT * grad_coef
    return jnp.concatenate(
        [
            scaled.reshape(-1),
            1.0 + DT - 2.0 * jnp.sum(scaled, axis=1),
            (DT * (composition - jnp.mean(composition, axis=0))).reshape(-1),
            DT * (latent - jnp.mean(latent)),
            (composition - composition[3]).reshape(-1),
            DT * diffusivity,
            1.0 - 6.0 * DT * diffusivity,
            melt_table.reshape(-1),
        ]
    )


class Round:
    def __init__(self, turn, place, sizes, table, levels):
        self.ng, self.block, self.rows = sizes
        self.table, self.levels = table, levels
        self.start = place * self.block + SHIFT * (turn + 1) - STEPS
        self.lowest = SHIFT * turn - self.start
        self.top = self.ng * self.block + SHIFT * turn - 1 - self.start

    def fill(self, source, sides, planes, to):
        def store(values, e, at, length):
            for f, value in zip(SENT, values):
                self.levels[0][f, e, at : at + length] = value
            self.levels[0][3, e, at : at + length] = 1.0 - values[0] - values[1] - values[2]

        @pl.loop(0, planes)
        def _(i):
            store([source[f, i] for f in range(len(SENT))], i + to, PAD, self.rows)

        for side, at, first in ((sides[0], PAD - STEPS, sides[2]), (sides[1], PAD + self.rows, sides[2])):

            @pl.loop(0, planes)
            def _(i, side=side, at=at, first=first):
                store([side[f, i + first] for f in range(len(SENT))], i + to, at, STEPS)

    def advance(self, src, e, at):
        table, window = self.table, pl.ds(at, 8)
        up, down = jnp.minimum(e + 1, self.top), jnp.maximum(e - 1, self.lowest)
        total = float(self.ng * self.block)
        theta = ((e + self.start).astype(jnp.float32) - 0.5 * total) / total
        mid = [src[f, e, window] for f in range(6)]
        gsum = [src[f, up, window] + src[f, down, window] for f in range(6)]
        xsum = [src[f, e, pl.ds(at + 1, 8)] + src[f, e, pl.ds(at - 1, 8)] for f in range(6)]
        ysum = [pltpu.roll(v, 1, 1) + pltpu.roll(v, v.shape[1] - 1, 1) for v in mid]
        spread = [
            table[GRAD + 3 * a] * gsum[a]
            + table[GRAD + 3 * a + 1] * xsum[a]
            + table[GRAD + 3 * a + 2] * ysum[a]
            + table[CENTER + a] * mid[a]
            for a in range(4)
        ]
        mean = 0.25 * (spread[0] + spread[1] + spread[2] + spread[3]) - 0.25
        trial = [
            spread[a]
            - mean
            - table[COUPLE + 2 * a] * mid[4]
            - table[COUPLE + 2 * a + 1] * mid[5]
            - table[LATENT + a] * theta
            for a in range(3)
        ]
        trial.append(1.0 - trial[0] - trial[1] - trial[2])
        clipped = [jnp.clip(t, 0.0, 1.0) for t in trial]
        inverse = 1.0 / (clipped[0] + clipped[1] + clipped[2] + clipped[3])
        new = [c * inverse for c in clipped]
        change = [n - v for n, v in zip(new[:3], mid[:3])]
        for k in range(2):
            release = table[RELEASE + k] * change[0]
            for a in range(1, 3):
                release = release + table[RELEASE + 2 * a + k] * change[a]
            sides = gsum[4 + k] + xsum[4 + k] + ysum[4 + k]
            new.append(table[SPREAD + k] * sides + table[STAY + k] * mid[4 + k] - release)
        return new

    def sweep(self, step, first, stop, write=None):
        src, dst = self.levels[step - 1], self.levels[step % STEPS]
        if write is None:
            tiles = [PAD - STEPS + 8 * t for t in range(self.rows // 8 + 1)]

            def write(e, at, new):
                for f in range(6):
                    dst[f, e, pl.ds(at, 8)] = new[f]

        else:
            tiles = [PAD + 8 * t for t in range(self.rows // 8)]

        @pl.loop(0, (stop - first) // PLANES)
        def _(i):
            for p in range(PLANES):
                e = first + PLANES * i + p
                for at in tiles:
                    write(e, at, self.advance(src, e, at))


def first_kernel(turn, place_of, sizes, table, own, left, right, early, seam, even, odd):
    run = Round(turn, place_of(), sizes, table, (even, odd, even, odd))
    kept = own.shape[1]
    run.fill(own, (left, right, 0), kept, 0)
    fields = range(6) if early.shape[0] == 6 else SENT

    def write(e, at, new):
        for i, f in enumerate(fields):
            early[i, e - STEPS, pl.ds(at - PAD, 8)] = new[f]

    for step in range(1, STEPS):
        run.sweep(step, step, kept - step)
        for plane in range(2):
            for f in range(6):
                seam[step - 1, f, plane] = run.levels[step][f, kept - step - 2 + plane]
    run.sweep(STEPS, STEPS, kept - STEPS, write)


def second_kernel(
    turn, place_of, sizes, last, table, own, left, right, seam, early, low, high, left2, right2, index, *rest
):
    outs, (even, odd) = rest[:-2], rest[-2:]
    place = place_of()
    run = Round(turn, place, sizes, table, (even, odd, even, odd))
    kept, lows, highs = own.shape[1], low.shape[1], high.shape[1]
    height = kept + lows + highs
    run.fill(own.at[:, pl.ds(kept - 2, 2)], (left, right, kept - 2), 2, kept - 2)
    run.fill(low, (left2, right2, 0), lows, kept)
    run.fill(high, (left2, right2, lows), highs, kept + lows)
    for step in range(1, STEPS):
        for plane in range(2):
            for f in range(6):
                run.levels[step][f, kept - step - 2 + plane] = seam[step - 1, f, plane]
    ready = early.shape[1]

    def write(climbs):
        def put(e, at, new):
            o, here = e - STEPS, pl.ds(at - PAD, 8)
            if last:
                for a in range(4):
                    outs[0][a, o, here] = new[a]
                for k in range(2):
                    outs[1][k, o, here] = new[4 + k]
                return
            for i, f in enumerate(SENT):
                outs[0][i, o - ready, here] = new[f]
                if climbs:
                    outs[1][i, o - ready, here] = new[f]

        return put

    if last:
        for a in range(4):
            outs[0][a, :ready] = early[a]
        for k in range(2):
            outs[1][k, :ready] = early[4 + k]
    for step in range(1, STEPS):
        run.sweep(step, kept - step, height - step)
    climbed = run.block if last else ready + outs[1].shape[1]
    run.sweep(STEPS, kept - STEPS, climbed + STEPS, write(True))
    if not last:
        run.sweep(STEPS, climbed + STEPS, height - STEPS, write(False))

    fresh = run.block - SHIFT

    @pl.when(place == run.ng - 1)
    def _():
        for j in range(SHIFT):
            put = write(fresh + j < climbed)
            for t in range(run.rows // 8):
                row = index[j, pl.ds(8 * t, 8)]
                mu = [jnp.zeros(row.shape, jnp.float32)] * 2
                for m in range((table.shape[0] - MELT) // 2):
                    mu = [jnp.where(row == m, table[MELT + 2 * m + k], mu[k]) for k in range(2)]
                none = jnp.zeros(row.shape, jnp.float32)
                put(fresh + j + STEPS, PAD + 8 * t, [none, none, none, none + 1.0] + mu)


def prepare_kernel(labels, roughness, potential, staying, low, high):
    lows, highs = low.shape[1], high.shape[1]

    def plane(o, kept):
        kind = labels[o]
        rough = [roughness[a, o] for a in range(4)]
        inverse = 1.0 / (3.0 + rough[0] + rough[1] + rough[2] + rough[3])
        new = [(jnp.where(kind == a, 3.0, 0.0) + rough[a]) * inverse for a in range(3)]
        new += [potential[0, o], potential[1, o]]
        for ref, at in kept:
            for f, value in enumerate(new):
                ref[f, at] = value

    @pl.loop(0, lows)
    def _(o):
        plane(o, [(low, o)])

    @pl.loop(lows, lows + highs)
    def _(o):
        plane(o, [(high, o - lows), (staying, o - lows)])

    @pl.loop(lows + highs, labels.shape[0])
    def _(o):
        plane(o, [(staying, o - lows)])


def on_device(ng, nl, labels, roughness, potential, grad_coef, composition, latent, diffusivity, melt_table, melt_index):
    block, rows, lanes = labels.shape
    vmem = pl.BlockSpec(memory_space=pltpu.VMEM)
    smem = pl.BlockSpec(memory_space=pltpu.SMEM)
    f32 = jnp.float32
    kept = block - SHIFT + STEPS
    lows = block - kept
    highs = SHIFT + STEPS - lows
    height = kept + lows + highs
    table = scalar_table(grad_coef, composition, latent, diffusivity, melt_table)

    def home(g, l):
        return g * nl + l

    def away(g, l):
        return (g // 2 * 2 + (l % 2 ^ (l // 2 % 2))) * nl + l // 2 * 2 + g % 2

    def home_place():
        return lax.axis_index("grow")

    def away_place():
        return lax.axis_index("grow") // 2 * 2 + lax.axis_index("lat") % 2

    blocks = [(g, l) for g in range(ng) for l in range(nl)]

    def moved(array, before, after, climb):
        route = [(before(g + climb, l), after(g, l)) for g, l in blocks if g + climb < ng]
        return lax.ppermute(array, AXES, route)

    def beside(parts, where):
        first = jnp.concatenate([p[:, :, :STEPS] for p in parts], axis=1)
        final = jnp.concatenate([p[:, :, rows - STEPS :] for p in parts], axis=1)
        left = lax.ppermute(final, AXES, [(where(g, l), where(g, (l + 1) % nl)) for g, l in blocks])
        right = lax.ppermute(first, AXES, [(where(g, (l + 1) % nl), where(g, l)) for g, l in blocks])
        return left, right

    def piece(planes, fields=len(SENT)):
        return jax.ShapeDtypeStruct((fields, planes, rows, lanes), f32)

    def cost(planes, moved_bytes):
        return pl.CostEstimate(flops=130 * 6 * planes * rows * lanes, bytes_accessed=moved_bytes, transcendentals=0)

    staying, low, high = pl.pallas_call(
        prepare_kernel,
        out_shape=[piece(n) for n in (kept, lows, highs)],
        in_specs=[vmem] * 3,
        out_specs=[vmem] * 3,
        name="prepare",
    )(labels, roughness, potential)

    away_index = lax.ppermute(
        melt_index[: ROUNDS - 1],
        AXES,
        [(home(ng - 1, l), away(ng - 1, l)) for l in range(nl)],
    )

    scratch = [pltpu.VMEM((6, height, rows + 2 * PAD, lanes), f32)] * 2
    params = pltpu.CompilerParams(vmem_limit_bytes=40 << 20)
    for turn in range(ROUNDS):
        last = turn == ROUNDS - 1
        before = home if turn == 0 else away
        after = home if last else away
        place_of = home_place if last else away_place
        own = staying if before is after else moved(staying, before, after, 0)
        low, high = moved(low, before, after, 1), moved(high, before, after, 1)
        left, right = beside([own], after)
        early, seam = pl.pallas_call(
            functools.partial(first_kernel, turn, place_of, (ng, block, rows)),
            out_shape=[piece(lows, 6 if last else len(SENT)), jax.ShapeDtypeStruct((STEPS - 1, 6, 2, rows + 2 * PAD, lanes), f32)],
            in_specs=[smem] + [vmem] * 3,
            out_specs=[vmem] * 2,
            scratch_shapes=scratch,
            compiler_params=params,
            cost_estimate=cost(28, 3000000),
            name="first",
        )(table, own, left, right)
        left2, right2 = beside([low, high], after)
        if last:
            shapes = [jax.ShapeDtypeStruct((n, block, rows, lanes), f32) for n in (4, 2)]
        else:
            shapes = [piece(kept), piece(highs)]
        outs = pl.pallas_call(
            functools.partial(second_kernel, turn, place_of, (ng, block, rows), last),
            out_shape=shapes,
            in_specs=[smem] + [vmem] * 10,
            out_specs=[vmem] * 2,
            scratch_shapes=scratch,
            compiler_params=params,
            cost_estimate=cost(48, 6000000),
            name="second",
        )(table, own, left, right, seam, early, low, high, left2, right2, melt_index[turn] if last else away_index[turn])
        staying, high = outs
        low = early
    return outs[0], outs[1]


def solution(mesh):
    ng, nl = mesh.shape["grow"], mesh.shape["lat"]
    placed = (
        P("grow", "lat", None),
        P(None, "grow", "lat", None),
        P(None, "grow", "lat", None),
        P(),
        P(),
        P(),
        P(),
        P(),
        P(None, None, "lat", None),
    )
    return jax.shard_map(
        functools.partial(on_device, ng, nl),
        mesh=mesh,
        in_specs=placed,
        out_specs=(P(None, "grow", "lat", None), P(None, "grow", "lat", None)),
        check_vma=False,
    )
```

```python
import functools

import jax
import jax.numpy as jnp
from jax import lax
from jax.experimental import pallas as pl
from jax.experimental.pallas import tpu as pltpu
from jax.sharding import PartitionSpec as P


STEPS = 4
ROUNDS = 4
SHIFT = 8
SENT = (0, 1, 2, 4, 5)
PAD = 8
DT = 0.04
PLANES = 2
AXES = ("grow", "lat")
GRAD, CENTER, COUPLE, LATENT, RELEASE, SPREAD, STAY, MELT = 0, 12, 16, 24, 28, 36, 38, 40


def scalar_table(grad_coef, composition, latent, diffusivity, melt_table):
    scaled = DT * grad_coef
    return jnp.concatenate(
        [
            scaled.reshape(-1),
            1.0 + DT - 2.0 * jnp.sum(scaled, axis=1),
            (DT * (composition - jnp.mean(composition, axis=0))).reshape(-1),
            DT * (latent - jnp.mean(latent)),
            (composition - composition[3]).reshape(-1),
            DT * diffusivity,
            1.0 - 6.0 * DT * diffusivity,
            melt_table.reshape(-1),
        ]
    )


class Round:
    def __init__(self, turn, place, sizes, table, levels):
        self.ng, self.block, self.rows = sizes
        self.table, self.levels = table, levels
        self.start = place * self.block + SHIFT * (turn + 1) - STEPS
        self.lowest = SHIFT * turn - self.start
        self.top = self.ng * self.block + SHIFT * turn - 1 - self.start

    def fill(self, source, sides, planes, to):
        def store(values, e, at, length):
            for f, value in zip(SENT, values):
                self.levels[0][f, e, at : at + length] = value
            self.levels[0][3, e, at : at + length] = 1.0 - values[0] - values[1] - values[2]

        @pl.loop(0, planes)
        def _(i):
            store([source[f, i] for f in range(len(SENT))], i + to, PAD, self.rows)

        for side, at, first in ((sides[0], PAD - STEPS, sides[2]), (sides[1], PAD + self.rows, sides[2])):

            @pl.loop(0, planes)
            def _(i, side=side, at=at, first=first):
                store([side[f, i + first] for f in range(len(SENT))], i + to, at, STEPS)

    def advance(self, src, e, at):
        table, window = self.table, pl.ds(at, 8)
        up, down = jnp.minimum(e + 1, self.top), jnp.maximum(e - 1, self.lowest)
        total = float(self.ng * self.block)
        theta = ((e + self.start).astype(jnp.float32) - 0.5 * total) / total
        mid = [src[f, e, window] for f in range(6)]
        gsum = [src[f, up, window] + src[f, down, window] for f in range(6)]
        xsum = [src[f, e, pl.ds(at + 1, 8)] + src[f, e, pl.ds(at - 1, 8)] for f in range(6)]
        ysum = [pltpu.roll(v, 1, 1) + pltpu.roll(v, v.shape[1] - 1, 1) for v in mid]
        spread = [
            table[GRAD + 3 * a] * gsum[a]
            + table[GRAD + 3 * a + 1] * xsum[a]
            + table[GRAD + 3 * a + 2] * ysum[a]
            + table[CENTER + a] * mid[a]
            for a in range(4)
        ]
        mean = 0.25 * (spread[0] + spread[1] + spread[2] + spread[3]) - 0.25
        trial = [
            spread[a]
            - mean
            - table[COUPLE + 2 * a] * mid[4]
            - table[COUPLE + 2 * a + 1] * mid[5]
            - table[LATENT + a] * theta
            for a in range(3)
        ]
        trial.append(1.0 - trial[0] - trial[1] - trial[2])
        clipped = [jnp.clip(t, 0.0, 1.0) for t in trial]
        inverse = 1.0 / (clipped[0] + clipped[1] + clipped[2] + clipped[3])
        new = [c * inverse for c in clipped]
        change = [n - v for n, v in zip(new[:3], mid[:3])]
        for k in range(2):
            release = table[RELEASE + k] * change[0]
            for a in range(1, 3):
                release = release + table[RELEASE + 2 * a + k] * change[a]
            sides = gsum[4 + k] + xsum[4 + k] + ysum[4 + k]
            new.append(table[SPREAD + k] * sides + table[STAY + k] * mid[4 + k] - release)
        return new

    def sweep(self, step, first, stop, write=None):
        src, dst = self.levels[step - 1], self.levels[step % STEPS]
        if write is None:
            tiles = [PAD - STEPS + 8 * t for t in range(self.rows // 8 + 1)]

            def write(e, at, new):
                for f in range(6):
                    dst[f, e, pl.ds(at, 8)] = new[f]

        else:
            tiles = [PAD + 8 * t for t in range(self.rows // 8)]

        @pl.loop(0, (stop - first) // PLANES)
        def _(i):
            for p in range(PLANES):
                e = first + PLANES * i + p
                for at in tiles:
                    write(e, at, self.advance(src, e, at))


def first_kernel(turn, place_of, sizes, table, own, left, right, early, seam, even, odd):
    run = Round(turn, place_of(), sizes, table, (even, odd, even, odd))
    kept = own.shape[1]
    run.fill(own, (left, right, 0), kept, 0)
    fields = range(6) if early.shape[0] == 6 else SENT

    def write(e, at, new):
        for i, f in enumerate(fields):
            early[i, e - STEPS, pl.ds(at - PAD, 8)] = new[f]

    for step in range(1, STEPS):
        run.sweep(step, step, kept - step)
        for plane in range(2):
            for f in range(6):
                seam[step - 1, f, plane] = run.levels[step][f, kept - step - 2 + plane]
    run.sweep(STEPS, STEPS, kept - STEPS, write)


def second_kernel(
    turn, place_of, sizes, last, table, own, left, right, seam, early, low, high, left2, right2, index, *rest
):
    outs, (even, odd) = rest[:-2], rest[-2:]
    place = place_of()
    run = Round(turn, place, sizes, table, (even, odd, even, odd))
    kept, lows, highs = own.shape[1], low.shape[1], high.shape[1]
    height = kept + lows + highs
    run.fill(own.at[:, pl.ds(kept - 2, 2)], (left, right, kept - 2), 2, kept - 2)
    run.fill(low, (left2, right2, 0), lows, kept)
    run.fill(high, (left2, right2, lows), highs, kept + lows)
    for step in range(1, STEPS):
        for plane in range(2):
            for f in range(6):
                run.levels[step][f, kept - step - 2 + plane] = seam[step - 1, f, plane]
    ready = early.shape[1]

    def write(climbs):
        def put(e, at, new):
            o, here = e - STEPS, pl.ds(at - PAD, 8)
            if last:
                for a in range(4):
                    outs[0][a, o, here] = new[a]
                for k in range(2):
                    outs[1][k, o, here] = new[4 + k]
                return
            for i, f in enumerate(SENT):
                outs[0][i, o - ready, here] = new[f]
                if climbs:
                    outs[1][i, o - ready, here] = new[f]

        return put

    if last:
        for a in range(4):
            outs[0][a, :ready] = early[a]
        for k in range(2):
            outs[1][k, :ready] = early[4 + k]
    for step in range(1, STEPS):
        run.sweep(step, kept - step, height - step)
    climbed = run.block if last else ready + outs[1].shape[1]
    run.sweep(STEPS, kept - STEPS, climbed + STEPS, write(True))
    if not last:
        run.sweep(STEPS, climbed + STEPS, height - STEPS, write(False))

    fresh = run.block - SHIFT

    @pl.when(place == run.ng - 1)
    def _():
        for j in range(SHIFT):
            put = write(fresh + j < climbed)
            for t in range(run.rows // 8):
                row = index[j, pl.ds(8 * t, 8)]
                mu = [jnp.zeros(row.shape, jnp.float32)] * 2
                for m in range((table.shape[0] - MELT) // 2):
                    mu = [jnp.where(row == m, table[MELT + 2 * m + k], mu[k]) for k in range(2)]
                none = jnp.zeros(row.shape, jnp.float32)
                put(fresh + j + STEPS, PAD + 8 * t, [none, none, none, none + 1.0] + mu)


def prepare_kernel(labels, roughness, potential, staying, low, high):
    lows, highs = low.shape[1], high.shape[1]

    def plane(o, kept):
        kind = labels[o]
        rough = [roughness[a, o] for a in range(4)]
        inverse = 1.0 / (3.0 + rough[0] + rough[1] + rough[2] + rough[3])
        new = [(jnp.where(kind == a, 3.0, 0.0) + rough[a]) * inverse for a in range(3)]
        new += [potential[0, o], potential[1, o]]
        for ref, at in kept:
            for f, value in enumerate(new):
                ref[f, at] = value

    @pl.loop(0, lows)
    def _(o):
        plane(o, [(low, o)])

    @pl.loop(lows, lows + highs)
    def _(o):
        plane(o, [(high, o - lows), (staying, o - lows)])

    @pl.loop(lows + highs, labels.shape[0])
    def _(o):
        plane(o, [(staying, o - lows)])


def on_device(ng, nl, labels, roughness, potential, grad_coef, composition, latent, diffusivity, melt_table, melt_index):
    block, rows, lanes = labels.shape
    vmem = pl.BlockSpec(memory_space=pltpu.VMEM)
    smem = pl.BlockSpec(memory_space=pltpu.SMEM)
    f32 = jnp.float32
    kept = block - SHIFT + STEPS
    lows = block - kept
    highs = SHIFT + STEPS - lows
    height = kept + lows + highs
    table = scalar_table(grad_coef, composition, latent, diffusivity, melt_table)

    def home(g, l):
        return g * nl + l

    def away(g, l):
        return (g // 2 * 2 + (l % 2 ^ (l // 2 % 2))) * nl + l // 2 * 2 + g % 2

    def home_place():
        return lax.axis_index("grow")

    def away_place():
        return lax.axis_index("grow") // 2 * 2 + lax.axis_index("lat") % 2

    blocks = [(g, l) for g in range(ng) for l in range(nl)]

    def moved(array, before, after, climb):
        route = [(before(g + climb, l), after(g, l)) for g, l in blocks if g + climb < ng]
        return lax.ppermute(array, AXES, route)

    def beside(parts, where):
        first = jnp.concatenate([p[:, :, :STEPS] for p in parts], axis=1)
        final = jnp.concatenate([p[:, :, rows - STEPS :] for p in parts], axis=1)
        left = lax.ppermute(final, AXES, [(where(g, l), where(g, (l + 1) % nl)) for g, l in blocks])
        right = lax.ppermute(first, AXES, [(where(g, (l + 1) % nl), where(g, l)) for g, l in blocks])
        return left, right

    def piece(planes, fields=len(SENT)):
        return jax.ShapeDtypeStruct((fields, planes, rows, lanes), f32)

    def cost(planes, moved_bytes):
        return pl.CostEstimate(flops=130 * 6 * planes * rows * lanes, bytes_accessed=moved_bytes, transcendentals=0)

    staying, low, high = pl.pallas_call(
        prepare_kernel,
        out_shape=[piece(n) for n in (kept, lows, highs)],
        in_specs=[vmem] * 3,
        out_specs=[vmem] * 3,
        name="prepare",
    )(labels, roughness, potential)

    away_index = lax.ppermute(
        melt_index[: ROUNDS - 1],
        AXES,
        [(home(ng - 1, l), away(ng - 1, l)) for l in range(nl)],
    )

    scratch = [pltpu.VMEM((6, height, rows + 2 * PAD, lanes), f32)] * 2
    params = pltpu.CompilerParams(vmem_limit_bytes=40 << 20)
    low = moved(low, home, away, 1)
    for turn in range(ROUNDS):
        last = turn == ROUNDS - 1
        before = home if turn == 0 else away
        after = home if last else away
        place_of = home_place if last else away_place
        own = staying if before is after else moved(staying, before, after, 0)
        high = moved(high, before, after, 1)
        left, right = beside([own], after)
        first = pl.pallas_call(
            functools.partial(first_kernel, turn, place_of, (ng, block, rows)),
            out_shape=[piece(lows, 6 if last else len(SENT)), jax.ShapeDtypeStruct((STEPS - 1, 6, 2, rows + 2 * PAD, lanes), f32)],
            in_specs=[smem] + [vmem] * 3,
            out_specs=[vmem] * 2,
            scratch_shapes=scratch,
            compiler_params=params,
            cost_estimate=cost(28, 3000000),
            name="first",
        )
        early, seam = first(table, own, left, right)
        if not last:
            to = home if turn == ROUNDS - 2 else away
            next_low = moved(early, away, to, 1)
        left2, right2 = beside([low, high], after)
        if last:
            shapes = [jax.ShapeDtypeStruct((n, block, rows, lanes), f32) for n in (4, 2)]
        else:
            shapes = [piece(kept), piece(highs)]
        second = pl.pallas_call(
            functools.partial(second_kernel, turn, place_of, (ng, block, rows), last),
            out_shape=shapes,
            in_specs=[smem] + [vmem] * 10,
            out_specs=[vmem] * 2,
            scratch_shapes=scratch,
            compiler_params=params,
            cost_estimate=cost(48, 6000000),
            name="second",
        )
        index = melt_index[turn] if last else away_index[turn]
        outs = second(table, own, left, right, seam, early, low, high, left2, right2, index)
        staying, high = outs
        low = next_low
    return outs[0], outs[1]


def solution(mesh):
    ng, nl = mesh.shape["grow"], mesh.shape["lat"]
    placed = (
        P("grow", "lat", None),
        P(None, "grow", "lat", None),
        P(None, "grow", "lat", None),
        P(),
        P(),
        P(),
        P(),
        P(),
        P(None, None, "lat", None),
    )
    return jax.shard_map(
        functools.partial(on_device, ng, nl),
        mesh=mesh,
        in_specs=placed,
        out_specs=(P(None, "grow", "lat", None), P(None, "grow", "lat", None)),
        check_vma=False,
    )
```

```python
import functools

import jax
import jax.numpy as jnp
from jax import lax
from jax.experimental import pallas as pl
from jax.experimental.pallas import tpu as pltpu
from jax.sharding import PartitionSpec as P


STEPS = 4
ROUNDS = 4
SHIFT = 8
SENT = (0, 1, 2, 4, 5)
PAD = 8
DT = 0.04
PLANES = 2
AXES = ("grow", "lat")
GRAD, CENTER, COUPLE, LATENT, RELEASE, SPREAD, STAY, MELT = 0, 12, 16, 24, 28, 36, 38, 40


def scalar_table(grad_coef, composition, latent, diffusivity, melt_table):
    scaled = DT * grad_coef
    return jnp.concatenate(
        [
            scaled.reshape(-1),
            1.0 + DT - 2.0 * jnp.sum(scaled, axis=1),
            (DT * (composition - jnp.mean(composition, axis=0))).reshape(-1),
            DT * (latent - jnp.mean(latent)),
            (composition - composition[3]).reshape(-1),
            DT * diffusivity,
            1.0 - 6.0 * DT * diffusivity,
            melt_table.reshape(-1),
        ]
    )


class Round:
    def __init__(self, turn, place, sizes, table, even, odd):
        self.ng, self.block, self.rows = sizes
        self.table, self.levels = table, (even, odd, even, odd)
        self.start = place * self.block + SHIFT * (turn + 1) - STEPS
        self.lowest = SHIFT * turn - self.start
        self.top = self.ng * self.block + SHIFT * turn - 1 - self.start

    def fill(self, source, halo, planes, to, halo_from=0):
        level = self.levels[0]

        @pl.loop(0, planes)
        def _(i):
            body = [source[f, i] for f in range(len(SENT))]
            side = [halo[f, i + halo_from] for f in range(len(SENT))]
            body.insert(3, 1.0 - body[0] - body[1] - body[2])
            side.insert(3, 1.0 - side[0] - side[1] - side[2])
            for f in range(6):
                level[f, i + to, PAD : PAD + self.rows] = body[f]
                level[f, i + to, PAD - STEPS : PAD] = side[f][:STEPS]
                level[f, i + to, PAD + self.rows : PAD + self.rows + STEPS] = side[f][STEPS:]

    def advance(self, src, e, at):
        table, window = self.table, pl.ds(at, 8)
        up, down = jnp.minimum(e + 1, self.top), jnp.maximum(e - 1, self.lowest)
        total = float(self.ng * self.block)
        theta = ((e + self.start).astype(jnp.float32) - 0.5 * total) / total
        mid = [src[f, e, window] for f in range(6)]
        gsum = [src[f, up, window] + src[f, down, window] for f in range(6)]
        xsum = [src[f, e, pl.ds(at + 1, 8)] + src[f, e, pl.ds(at - 1, 8)] for f in range(6)]
        ysum = [pltpu.roll(v, 1, 1) + pltpu.roll(v, v.shape[1] - 1, 1) for v in mid]
        spread = [
            table[GRAD + 3 * a] * gsum[a]
            + table[GRAD + 3 * a + 1] * xsum[a]
            + table[GRAD + 3 * a + 2] * ysum[a]
            + table[CENTER + a] * mid[a]
            for a in range(4)
        ]
        mean = 0.25 * (spread[0] + spread[1] + spread[2] + spread[3]) - 0.25
        trial = [
            spread[a]
            - mean
            - table[COUPLE + 2 * a] * mid[4]
            - table[COUPLE + 2 * a + 1] * mid[5]
            - table[LATENT + a] * theta
            for a in range(3)
        ]
        trial.append(1.0 - trial[0] - trial[1] - trial[2])
        clipped = [jnp.clip(t, 0.0, 1.0) for t in trial]
        inverse = 1.0 / (clipped[0] + clipped[1] + clipped[2] + clipped[3])
        new = [c * inverse for c in clipped]
        change = [n - v for n, v in zip(new[:3], mid[:3])]
        for k in range(2):
            release = table[RELEASE + k] * change[0]
            for a in range(1, 3):
                release = release + table[RELEASE + 2 * a + k] * change[a]
            sides = gsum[4 + k] + xsum[4 + k] + ysum[4 + k]
            new.append(table[SPREAD + k] * sides + table[STAY + k] * mid[4 + k] - release)
        return new

    def sweep(self, step, first, stop, write=None):
        src, dst = self.levels[step - 1], self.levels[step % STEPS]
        if write is None:
            tiles = [PAD - STEPS + 8 * t for t in range(self.rows // 8 + 1)]

            def write(e, at, new):
                for f in range(6):
                    dst[f, e, pl.ds(at, 8)] = new[f]

        else:
            tiles = [PAD + 8 * t for t in range(self.rows // 8)]

        @pl.loop(0, (stop - first) // PLANES)
        def _(i):
            for p in range(PLANES):
                e = first + PLANES * i + p
                for at in tiles:
                    write(e, at, self.advance(src, e, at))


def part_kernel(turn, place_of, sizes, begin, parts, has_seam, gives_seam, first_out, fresh, table, *refs):
    refs, (even, odd) = list(refs[:-2]), refs[-2:]
    place = place_of()
    run = Round(turn, place, sizes, table, even, odd)
    end = begin
    seam = refs.pop(0) if has_seam else None
    index = refs.pop(0) if fresh else None
    for planes, halo_from in parts:
        if halo_from == 0:
            source, halo = refs.pop(0), refs.pop(0)
        else:
            source = refs.pop(0)
        run.fill(source, halo, planes, end, halo_from)
        end += planes
    next_seam = refs.pop() if gives_seam else None
    outs = refs

    def bounds(step):
        return (begin if has_seam else 2 * step) - step, end - step

    for level in range(STEPS):
        if has_seam:
            for plane in range(2):
                for f in range(6):
                    run.levels[level][f, begin - level - 2 + plane] = seam[level, f, plane]

    def hold(level):
        if gives_seam:
            for plane in range(2):
                for f in range(6):
                    next_seam[level, f, plane] = run.levels[level][f, end - level - 2 + plane]

    def write(targets):
        def put(e, at, new):
            for ref in targets:
                for i, f in enumerate(SENT):
                    ref[i, e - STEPS - first_out, pl.ds(at - PAD, 8)] = new[f]

        return put

    hold(0)
    for step in range(1, STEPS):
        run.sweep(step, *bounds(step))
        hold(step)
    first, last = bounds(STEPS)
    ends = [first_out + STEPS + ref.shape[1] for ref in outs]
    marks = sorted(set([first, last] + [m for m in ends if first < m < last]))
    for low, high in zip(marks, marks[1:]):
        run.sweep(STEPS, low, high, write([ref for ref, m in zip(outs, ends) if m >= high]))

    if fresh:

        @pl.when(place == run.ng - 1)
        def _():
            for j in range(SHIFT):
                e = run.block - SHIFT + j + STEPS
                put = write([ref for ref, m in zip(outs, ends) if m > e])
                for t in range(run.rows // 8):
                    put(e, PAD + 8 * t, melt(table, index[j, pl.ds(8 * t, 8)]))


def melt(table, row):
    mu = [jnp.zeros(row.shape, jnp.float32)] * 2
    for m in range((table.shape[0] - MELT) // 2):
        mu = [jnp.where(row == m, table[MELT + 2 * m + k], mu[k]) for k in range(2)]
    none = jnp.zeros(row.shape, jnp.float32)
    return [none, none, none, none + 1.0] + mu


def finish_kernel(place_of, ng, table, index, *refs):
    pieces, (phases, potentials) = refs[:-2], refs[-2:]

    def put(o, here, new):
        for a in range(4):
            phases[a, o, here] = new[a]
        for k in range(2):
            potentials[k, o, here] = new[4 + k]

    at = 0
    for part in pieces:

        @pl.loop(0, part.shape[1])
        def _(i, part=part, at=at):
            new = [part[f, i] for f in range(len(SENT))]
            new.insert(3, 1.0 - new[0] - new[1] - new[2])
            put(i + at, slice(None), new)

        at += part.shape[1]

    @pl.when(place_of() == ng - 1)
    def _():
        for j in range(SHIFT):
            for t in range(index.shape[1] // 8):
                here = pl.ds(8 * t, 8)
                put(at - SHIFT + j, here, melt(table, index[j, here]))


def prepare_kernel(labels, roughness, potential, low, high, staying):
    lows, highs = low.shape[1], high.shape[1]

    def plane(o, kept):
        kind = labels[o]
        rough = [roughness[a, o] for a in range(4)]
        inverse = 1.0 / (3.0 + rough[0] + rough[1] + rough[2] + rough[3])
        new = [(jnp.where(kind == a, 3.0, 0.0) + rough[a]) * inverse for a in range(3)]
        new += [potential[0, o], potential[1, o]]
        for ref, at in kept:
            for f, value in enumerate(new):
                ref[f, at] = value

    @pl.loop(0, lows)
    def _(o):
        plane(o, [(low, o)])

    @pl.loop(lows, lows + highs)
    def _(o):
        plane(o, [(high, o - lows), (staying, o - lows)])

    @pl.loop(lows + highs, labels.shape[0])
    def _(o):
        plane(o, [(staying, o - lows)])


def on_device(ng, nl, labels, roughness, potential, grad_coef, composition, latent, diffusivity, melt_table, melt_index):
    block, rows, lanes = labels.shape
    vmem = pl.BlockSpec(memory_space=pltpu.VMEM)
    smem = pl.BlockSpec(memory_space=pltpu.SMEM)
    f32 = jnp.float32
    kept = block - SHIFT + STEPS
    lows = block - kept
    highs = SHIFT + STEPS - lows
    height = kept + lows + highs
    table = scalar_table(grad_coef, composition, latent, diffusivity, melt_table)

    def home(g, l):
        return g * nl + l

    def away(g, l):
        return (g // 2 * 2 + (l % 2 ^ (l // 2 % 2))) * nl + l // 2 * 2 + g % 2

    def home_place():
        return lax.axis_index("grow")

    def away_place():
        return lax.axis_index("grow") // 2 * 2 + lax.axis_index("lat") % 2

    blocks = [(g, l) for g in range(ng) for l in range(nl)]

    def moved(array, before, after, climb):
        route = [(before(g + climb, l), after(g, l)) for g, l in blocks if g + climb < ng]
        return lax.ppermute(array, AXES, route)

    def beside(parts, where):
        first = jnp.concatenate([p[:, :, :STEPS] for p in parts], axis=1)
        final = jnp.concatenate([p[:, :, rows - STEPS :] for p in parts], axis=1)
        left = lax.ppermute(final, AXES, [(where(g, l), where(g, (l + 1) % nl)) for g, l in blocks])
        right = lax.ppermute(first, AXES, [(where(g, (l + 1) % nl), where(g, l)) for g, l in blocks])
        return left, right

    def piece(planes, width=rows):
        return jax.ShapeDtypeStruct((len(SENT), planes, width, lanes), f32)

    def cost(planes, moved_bytes):
        return pl.CostEstimate(flops=130 * 6 * planes * rows * lanes, bytes_accessed=moved_bytes, transcendentals=0)

    seam_shape = jax.ShapeDtypeStruct((STEPS, 6, 2, rows + 2 * PAD, lanes), f32)
    scratch = [pltpu.VMEM((6, height, rows + 2 * PAD, lanes), f32)] * 2

    def part(turn, begin, planes, has_seam, gives_seam, first_out, sent, *args, fresh=False):
        size = sum(n for n, _ in planes)
        return pl.pallas_call(
            functools.partial(
                part_kernel, turn, away_place, (ng, block, rows), begin, planes, has_seam, gives_seam, first_out, fresh
            ),
            out_shape=[piece(n) for n in sent] + [seam_shape] * gives_seam,
            in_specs=[smem] + [vmem] * len(args),
            out_specs=[vmem] * (len(sent) + gives_seam),
            scratch_shapes=scratch,
            compiler_params=pltpu.CompilerParams(vmem_limit_bytes=40 << 20),
            cost_estimate=cost(4 * size, 4000000),
            name="part",
        )(table, *args)

    low, high, staying = pl.pallas_call(
        prepare_kernel,
        out_shape=[piece(n) for n in (lows, highs, kept)],
        in_specs=[vmem] * 3,
        out_specs=[vmem] * 3,
        name="prepare",
    )(labels, roughness, potential)

    away_index = lax.ppermute(
        melt_index[: ROUNDS - 1],
        AXES,
        [(home(ng - 1, l), away(ng - 1, l)) for l in range(nl)],
    )

    early = low
    for turn in range(ROUNDS):
        last = turn == ROUNDS - 1
        before = home if turn == 0 else away
        left, right = beside([early, staying], before)
        own_halo = jnp.concatenate([left[:, lows:], right[:, lows:]], axis=2)
        halo = jnp.concatenate([left[:, : lows + highs], right[:, : lows + highs]], axis=2)
        if turn == 0:
            staying = moved(staying, before, away, 0)
            own_halo = moved(own_halo, before, away, 0)
            low = moved(low, before, away, 1)
        high = moved(high, before, away, 1)
        halo = moved(halo, before, away, 1)
        early, seam = part(turn, 0, [(kept, 0)], False, True, 0, [lows], staying, own_halo)
        next_low = moved(early, away, home if last else away, 0 if last else 1)
        if last:
            break
        staying, high = functools.partial(part, fresh=True)(
            turn,
            kept,
            [(lows, 0), (highs, lows)],
            True,
            False,
            lows,
            [kept, highs],
            seam,
            away_index[turn],
            low,
            halo,
            high,
        )
        low = next_low

    cut = 2
    middle, seam = part(
        turn, kept, [(lows, 0), (cut, lows)], True, True, lows, [lows + cut], seam, low, halo, high[:, :cut]
    )
    middle = moved(middle, away, home, 0)
    (final,) = part(
        turn,
        kept + lows + cut,
        [(highs - cut, 0)],
        True,
        False,
        2 * lows + cut,
        [highs - cut],
        seam,
        high[:, cut:],
        halo[:, lows + cut :],
    )
    final = moved(final, away, home, 0)
    return pl.pallas_call(
        functools.partial(finish_kernel, home_place, ng),
        out_shape=[jax.ShapeDtypeStruct((n, block, rows, lanes), f32) for n in (4, 2)],
        in_specs=[smem] + [vmem] * 4,
        out_specs=[vmem] * 2,
        name="finish",
    )(table, melt_index[turn], next_low, middle, final)


def solution(mesh):
    ng, nl = mesh.shape["grow"], mesh.shape["lat"]
    placed = (
        P("grow", "lat", None),
        P(None, "grow", "lat", None),
        P(None, "grow", "lat", None),
        P(),
        P(),
        P(),
        P(),
        P(),
        P(None, None, "lat", None),
    )
    return jax.shard_map(
        functools.partial(on_device, ng, nl),
        mesh=mesh,
        in_specs=placed,
        out_specs=(P(None, "grow", "lat", None), P(None, "grow", "lat", None)),
        check_vma=False,
    )
```

```python
import functools

import jax
import jax.numpy as jnp
from jax import lax
from jax.experimental import pallas as pl
from jax.experimental.pallas import tpu as pltpu
from jax.sharding import PartitionSpec as P


STEPS = 4
ROUNDS = 4
SHIFT = 8
SENT = (0, 1, 2, 4, 5)
PAD = 8
DT = 0.04
PLANES = (2, 1)
AXES = ("grow", "lat")
GRAD, CENTER, COUPLE, LATENT, RELEASE, SPREAD, STAY, MELT = 0, 12, 16, 24, 28, 36, 38, 40


def scalar_table(grad_coef, composition, latent, diffusivity, melt_table):
    scaled = DT * grad_coef
    return jnp.concatenate(
        [
            scaled.reshape(-1),
            1.0 + DT - 2.0 * jnp.sum(scaled, axis=1),
            (DT * (composition - jnp.mean(composition, axis=0))).reshape(-1),
            DT * (latent - jnp.mean(latent)),
            (composition - composition[3]).reshape(-1),
            DT * diffusivity,
            1.0 - 6.0 * DT * diffusivity,
            melt_table.reshape(-1),
        ]
    )


class Round:
    def __init__(self, turn, place, sizes, table, even, odd):
        self.ng, self.block, self.rows = sizes
        self.table, self.levels = table, (even, odd, even, odd)
        self.start = place * self.block + SHIFT * (turn + 1) - STEPS
        self.lowest = SHIFT * turn - self.start
        self.top = self.ng * self.block + SHIFT * turn - 1 - self.start

    def fill(self, source, halo, planes, to, halo_from=0):
        level = self.levels[0]

        @pl.loop(0, planes)
        def _(i):
            body = [source[f, i] for f in range(len(SENT))]
            side = [halo[f, i + halo_from] for f in range(len(SENT))]
            body.insert(3, 1.0 - body[0] - body[1] - body[2])
            side.insert(3, 1.0 - side[0] - side[1] - side[2])
            for f in range(6):
                level[f, i + to, PAD : PAD + self.rows] = body[f]
                level[f, i + to, PAD - STEPS : PAD] = side[f][:STEPS]
                level[f, i + to, PAD + self.rows : PAD + self.rows + STEPS] = side[f][STEPS:]

    def advance(self, src, e, at):
        table, window = self.table, pl.ds(at, 8)
        up, down = jnp.minimum(e + 1, self.top), jnp.maximum(e - 1, self.lowest)
        total = float(self.ng * self.block)
        theta = ((e + self.start).astype(jnp.float32) - 0.5 * total) / total
        mid = [src[f, e, window] for f in range(6)]
        gsum = [src[f, up, window] + src[f, down, window] for f in range(6)]
        xsum = [src[f, e, pl.ds(at + 1, 8)] + src[f, e, pl.ds(at - 1, 8)] for f in range(6)]
        ysum = [pltpu.roll(v, 1, 1) + pltpu.roll(v, v.shape[1] - 1, 1) for v in mid]
        spread = [
            table[GRAD + 3 * a] * gsum[a]
            + table[GRAD + 3 * a + 1] * xsum[a]
            + table[GRAD + 3 * a + 2] * ysum[a]
            + table[CENTER + a] * mid[a]
            for a in range(4)
        ]
        mean = 0.25 * (spread[0] + spread[1] + spread[2] + spread[3]) - 0.25
        trial = [
            spread[a]
            - mean
            - table[COUPLE + 2 * a] * mid[4]
            - table[COUPLE + 2 * a + 1] * mid[5]
            - table[LATENT + a] * theta
            for a in range(3)
        ]
        trial.append(1.0 - trial[0] - trial[1] - trial[2])
        clipped = [jnp.clip(t, 0.0, 1.0) for t in trial]
        inverse = 1.0 / (clipped[0] + clipped[1] + clipped[2] + clipped[3])
        new = [c * inverse for c in clipped]
        change = [n - v for n, v in zip(new[:3], mid[:3])]
        for k in range(2):
            release = table[RELEASE + k] * change[0]
            for a in range(1, 3):
                release = release + table[RELEASE + 2 * a + k] * change[a]
            sides = gsum[4 + k] + xsum[4 + k] + ysum[4 + k]
            new.append(table[SPREAD + k] * sides + table[STAY + k] * mid[4 + k] - release)
        return new

    def sweep(self, step, first, stop, write=None):
        src, dst = self.levels[step - 1], self.levels[step % STEPS]
        if write is None:
            tiles = [PAD - STEPS + 8 * t for t in range(self.rows // 8 + 1)]

            def write(e, at, new):
                for f in range(6):
                    dst[f, e, pl.ds(at, 8)] = new[f]

        else:
            tiles = [PAD + 8 * t for t in range(self.rows // 8)]

        many = next(n for n in PLANES if (stop - first) % n == 0)

        @pl.loop(0, (stop - first) // many)
        def _(i):
            for p in range(many):
                e = first + many * i + p
                for at in tiles:
                    write(e, at, self.advance(src, e, at))


def part_kernel(turn, place_of, sizes, begin, parts, has_seam, gives_seam, out_from, fresh, table, *refs):
    refs, (even, odd) = list(refs[:-2]), refs[-2:]
    place = place_of()
    run = Round(turn, place, sizes, table, even, odd)
    end = begin
    seam = refs.pop(0) if has_seam else None
    index = refs.pop(0) if fresh else None
    halo = refs.pop(0)
    for planes, halo_from in parts:
        run.fill(refs.pop(0), halo, planes, end, halo_from)
        end += planes
    next_seam = refs.pop() if gives_seam else None
    outs = [(ref, o + STEPS, o + STEPS + ref.shape[1]) for ref, o in zip(refs, out_from)]

    def bounds(step):
        return (begin if has_seam else 2 * step) - step, end - step

    def hold(level):
        if gives_seam:
            for plane in range(2):
                for f in range(6):
                    next_seam[level, f, plane] = run.levels[level][f, end - level - 2 + plane]

    def write(first, stop):
        targets = [(ref, at) for ref, at, until in outs if at <= first and stop <= until]

        def put(e, at, new):
            for ref, origin in targets:
                for i, f in enumerate(SENT):
                    ref[i, e - origin, pl.ds(at - PAD, 8)] = new[f]

        return put

    if has_seam:
        for level in range(STEPS):
            for plane in range(2):
                for f in range(6):
                    run.levels[level][f, begin - level - 2 + plane] = seam[level, f, plane]
    hold(0)
    for step in range(1, STEPS):
        run.sweep(step, *bounds(step))
        hold(step)
    marks = sorted(set(bounds(STEPS)) | set(m for _, *ends in outs for m in ends))
    for first, stop in zip(marks, marks[1:]):
        run.sweep(STEPS, first, stop, write(first, stop))

    if fresh:

        @pl.when(place == run.ng - 1)
        def _():
            for j in range(SHIFT):
                e = run.block - SHIFT + j + STEPS
                if any(at <= e < until for _, at, until in outs):
                    for t in range(run.rows // 8):
                        write(e, e + 1)(e, PAD + 8 * t, melt(table, index[j, pl.ds(8 * t, 8)]))


def melt(table, row):
    mu = [jnp.zeros(row.shape, jnp.float32)] * 2
    for m in range((table.shape[0] - MELT) // 2):
        mu = [jnp.where(row == m, table[MELT + 2 * m + k], mu[k]) for k in range(2)]
    none = jnp.zeros(row.shape, jnp.float32)
    return [none, none, none, none + 1.0] + mu


def finish_kernel(place_of, ng, table, index, *refs):
    pieces, (phases, potentials) = refs[:-2], refs[-2:]

    def put(o, here, new):
        for a in range(4):
            phases[a, o, here] = new[a]
        for k in range(2):
            potentials[k, o, here] = new[4 + k]

    at = 0
    for part in pieces:

        @pl.loop(0, part.shape[1])
        def _(i, part=part, at=at):
            new = [part[f, i] for f in range(len(SENT))]
            new.insert(3, 1.0 - new[0] - new[1] - new[2])
            put(i + at, slice(None), new)

        at += part.shape[1]

    @pl.when(place_of() == ng - 1)
    def _():
        for j in range(SHIFT):
            for t in range(index.shape[1] // 8):
                here = pl.ds(8 * t, 8)
                put(at - SHIFT + j, here, melt(table, index[j, here]))


def prepare_kernel(labels, roughness, potential, *outs):
    starts = (0, outs[0].shape[1], labels.shape[0] - outs[2].shape[1])
    ranges = [(ref, at, at + ref.shape[1]) for ref, at in zip(outs, starts)]
    marks = sorted(set(m for _, *ends in ranges for m in ends))
    for first, stop in zip(marks, marks[1:]):
        targets = [(ref, at) for ref, at, until in ranges if at <= first and stop <= until]

        @pl.loop(first, stop)
        def _(o, targets=targets):
            kind = labels[o]
            rough = [roughness[a, o] for a in range(4)]
            inverse = 1.0 / (3.0 + rough[0] + rough[1] + rough[2] + rough[3])
            new = [(jnp.where(kind == a, 3.0, 0.0) + rough[a]) * inverse for a in range(3)]
            new += [potential[0, o], potential[1, o]]
            for ref, at in targets:
                for f, value in enumerate(new):
                    ref[f, o - at] = value


def on_device(ng, nl, labels, roughness, potential, grad_coef, composition, latent, diffusivity, melt_table, melt_index):
    block, rows, lanes = labels.shape
    vmem = pl.BlockSpec(memory_space=pltpu.VMEM)
    smem = pl.BlockSpec(memory_space=pltpu.SMEM)
    f32 = jnp.float32
    kept = block - SHIFT + STEPS
    lows = block - kept
    highs = SHIFT + STEPS - lows
    height = kept + lows + highs
    table = scalar_table(grad_coef, composition, latent, diffusivity, melt_table)

    def home(g, l):
        return g * nl + l

    def away(g, l):
        return (g // 2 * 2 + (l % 2 ^ (l // 2 % 2))) * nl + l // 2 * 2 + g % 2

    def home_place():
        return lax.axis_index("grow")

    def away_place():
        return lax.axis_index("grow") // 2 * 2 + lax.axis_index("lat") % 2

    blocks = [(g, l) for g in range(ng) for l in range(nl)]

    def moved(array, before, after, climb):
        route = [(before(g + climb, l), after(g, l)) for g, l in blocks if g + climb < ng]
        return lax.ppermute(array, AXES, route)

    def beside(parts, where):
        first = jnp.concatenate([p[:, :, :STEPS] for p in parts], axis=1)
        final = jnp.concatenate([p[:, :, rows - STEPS :] for p in parts], axis=1)
        left = lax.ppermute(final, AXES, [(where(g, l), where(g, (l + 1) % nl)) for g, l in blocks])
        right = lax.ppermute(first, AXES, [(where(g, (l + 1) % nl), where(g, l)) for g, l in blocks])
        return left, right

    def piece(planes, width=rows):
        return jax.ShapeDtypeStruct((len(SENT), planes, width, lanes), f32)

    def cost(planes, moved_bytes):
        return pl.CostEstimate(flops=130 * 6 * planes * rows * lanes, bytes_accessed=moved_bytes, transcendentals=0)

    seam_shape = jax.ShapeDtypeStruct((STEPS, 6, 2, rows + 2 * PAD, lanes), f32)
    scratch = [pltpu.VMEM((6, height, rows + 2 * PAD, lanes), f32)] * 2

    def limit(size):
        return pltpu.CompilerParams(vmem_limit_bytes=size << 20)

    def part(turn, begin, planes, has_seam, gives_seam, sent, fresh, *args):
        size = sum(n for n, _ in planes)
        return pl.pallas_call(
            functools.partial(
                part_kernel,
                turn,
                away_place,
                (ng, block, rows),
                begin,
                planes,
                has_seam,
                gives_seam,
                [o for o, _ in sent],
                fresh,
            ),
            out_shape=[piece(n) for _, n in sent] + [seam_shape] * gives_seam,
            in_specs=[smem] + [vmem] * len(args),
            out_specs=[vmem] * (len(sent) + gives_seam),
            scratch_shapes=scratch,
            compiler_params=limit(24),
            cost_estimate=cost(4 * size, 4000000),
            name="part",
        )(table, *args)

    front, back, own = pl.pallas_call(
        prepare_kernel,
        out_shape=[piece(n) for n in (highs, lows, kept)],
        in_specs=[vmem] * 3,
        out_specs=[vmem] * 3,
        compiler_params=limit(8),
        name="prepare",
    )(labels, roughness, potential)

    def packed(left, right, first, stop):
        return jnp.concatenate([left[:, first:stop], right[:, first:stop]], axis=2)

    own_parts = [(kept, 0)]
    left, right = beside([front[:, :lows], own], home)
    own = [moved(own, home, away, 0)]
    own_halo = moved(packed(left, right, lows, block), home, away, 0)
    front = moved(front, home, away, 1)
    halo = moved(packed(left, right, 0, lows + highs), home, away, 1)
    back = moved(back, home, away, 1)
    away_index = lax.ppermute(
        melt_index[: ROUNDS - 1], AXES, [(home(ng - 1, l), away(ng - 1, l)) for l in range(nl)]
    )
    early, seam = part(0, 0, own_parts, False, True, [(0, lows)], False, own_halo, *own)
    low = moved(early, away, away, 1)
    high, seam = part(
        0, kept, [(highs, 0)], True, True, [(lows, highs)], True, seam, away_index[0], halo, front
    )
    above = moved(high, away, away, 1)
    (rest,) = part(
        0,
        kept + highs,
        [(lows, highs)],
        True,
        False,
        [(lows + highs, lows)],
        True,
        seam,
        away_index[0],
        halo,
        back,
    )

    own_parts = [(highs, 0), (lows, highs)]
    for turn in range(1, ROUNDS):
        last = turn == ROUNDS - 1
        left, right = beside([early, high, rest], away)
        own, own_halo = [high, rest], packed(left, right, lows, block)
        if turn > 1:
            above = moved(high, away, away, 1)
        halo = moved(packed(left, right, 0, lows + highs), away, away, 1)
        early, seam = part(turn, 0, own_parts, False, True, [(0, lows)], False, own_halo, *own)
        sent = moved(early, away, home if last else away, 0 if last else 1)
        if last:
            break
        high, rest = part(
            turn,
            kept,
            [(lows, 0), (highs, lows)],
            True,
            False,
            [(lows, highs), (lows + highs, lows)],
            True,
            seam,
            away_index[turn],
            halo,
            low,
            above,
        )
        low = sent

    cut = 2
    middle, seam = part(
        turn,
        kept,
        [(lows, 0), (cut, lows)],
        True,
        True,
        [(lows, lows + cut)],
        False,
        seam,
        halo,
        low,
        above[:, :cut],
    )
    middle = moved(middle, away, home, 0)
    (final,) = part(
        turn,
        kept + lows + cut,
        [(highs - cut, lows + cut)],
        True,
        False,
        [(2 * lows + cut, highs - cut)],
        False,
        seam,
        halo,
        above[:, cut:],
    )
    final = moved(final, away, home, 0)
    return pl.pallas_call(
        functools.partial(finish_kernel, home_place, ng),
        out_shape=[jax.ShapeDtypeStruct((n, block, rows, lanes), f32) for n in (4, 2)],
        in_specs=[smem] + [vmem] * 4,
        out_specs=[vmem] * 2,
        compiler_params=limit(8),
        name="finish",
    )(table, melt_index[turn], sent, middle, final)


def solution(mesh):
    ng, nl = mesh.shape["grow"], mesh.shape["lat"]
    placed = (
        P("grow", "lat", None),
        P(None, "grow", "lat", None),
        P(None, "grow", "lat", None),
        P(),
        P(),
        P(),
        P(),
        P(),
        P(None, None, "lat", None),
    )
    return jax.shard_map(
        functools.partial(on_device, ng, nl),
        mesh=mesh,
        in_specs=placed,
        out_specs=(P(None, "grow", "lat", None), P(None, "grow", "lat", None)),
        check_vma=False,
    )
```

```python
import functools

import jax
import jax.numpy as jnp
from jax import lax
from jax.experimental import pallas as pl
from jax.experimental.pallas import tpu as pltpu
from jax.sharding import PartitionSpec as P


STEPS = 4
ROUNDS = 4
SHIFT = 8
SENT = (0, 1, 2, 4, 5)
PAD = 8
DT = 0.04
PLANES = (2, 1)
AXES = ("grow", "lat")
GRAD, CENTER, COUPLE, LATENT, RELEASE, SPREAD, STAY, MELT = 0, 12, 16, 24, 28, 36, 38, 40


def scalar_table(grad_coef, composition, latent, diffusivity, melt_table):
    scaled = DT * grad_coef
    return jnp.concatenate(
        [
            scaled.reshape(-1),
            1.0 + DT - 2.0 * jnp.sum(scaled, axis=1),
            (DT * (composition - jnp.mean(composition, axis=0))).reshape(-1),
            DT * (latent - jnp.mean(latent)),
            (composition - composition[3]).reshape(-1),
            DT * diffusivity,
            1.0 - 6.0 * DT * diffusivity,
            melt_table.reshape(-1),
        ]
    )


class Round:
    def __init__(self, turn, place, sizes, table, even, odd):
        self.ng, self.block, self.rows = sizes
        self.table, self.levels = table, (even, odd, even, odd)
        self.start = place * self.block + SHIFT * (turn + 1) - STEPS
        self.lowest = SHIFT * turn - self.start
        self.top = self.ng * self.block + SHIFT * turn - 1 - self.start

    def fill(self, source, halo, planes, to, halo_from=0):
        level = self.levels[0]

        @pl.loop(0, planes)
        def _(i):
            body = [source[f, i] for f in range(len(SENT))]
            side = [halo[f, i + halo_from] for f in range(len(SENT))]
            body.insert(3, 1.0 - body[0] - body[1] - body[2])
            side.insert(3, 1.0 - side[0] - side[1] - side[2])
            for f in range(6):
                level[f, i + to, PAD : PAD + self.rows] = body[f]
                level[f, i + to, PAD - STEPS : PAD] = side[f][:STEPS]
                level[f, i + to, PAD + self.rows : PAD + self.rows + STEPS] = side[f][STEPS:]

    def advance(self, src, e, at):
        table, window = self.table, pl.ds(at, 8)
        up, down = jnp.minimum(e + 1, self.top), jnp.maximum(e - 1, self.lowest)
        total = float(self.ng * self.block)
        theta = ((e + self.start).astype(jnp.float32) - 0.5 * total) / total
        mid = [src[f, e, window] for f in range(6)]
        gsum = [src[f, up, window] + src[f, down, window] for f in range(6)]
        xsum = [src[f, e, pl.ds(at + 1, 8)] + src[f, e, pl.ds(at - 1, 8)] for f in range(6)]
        ysum = [pltpu.roll(v, 1, 1) + pltpu.roll(v, v.shape[1] - 1, 1) for v in mid]
        spread = [
            table[GRAD + 3 * a] * gsum[a]
            + table[GRAD + 3 * a + 1] * xsum[a]
            + table[GRAD + 3 * a + 2] * ysum[a]
            + table[CENTER + a] * mid[a]
            for a in range(4)
        ]
        mean = 0.25 * (spread[0] + spread[1] + spread[2] + spread[3]) - 0.25
        trial = [
            spread[a]
            - mean
            - table[COUPLE + 2 * a] * mid[4]
            - table[COUPLE + 2 * a + 1] * mid[5]
            - table[LATENT + a] * theta
            for a in range(3)
        ]
        trial.append(1.0 - trial[0] - trial[1] - trial[2])
        clipped = [jnp.clip(t, 0.0, 1.0) for t in trial]
        inverse = 1.0 / (clipped[0] + clipped[1] + clipped[2] + clipped[3])
        new = [c * inverse for c in clipped]
        change = [n - v for n, v in zip(new[:3], mid[:3])]
        for k in range(2):
            release = table[RELEASE + k] * change[0]
            for a in range(1, 3):
                release = release + table[RELEASE + 2 * a + k] * change[a]
            sides = gsum[4 + k] + xsum[4 + k] + ysum[4 + k]
            new.append(table[SPREAD + k] * sides + table[STAY + k] * mid[4 + k] - release)
        return new

    def sweep(self, step, first, stop, write=None):
        src, dst = self.levels[step - 1], self.levels[step % STEPS]
        if write is None:
            tiles = [PAD - STEPS + 8 * t for t in range(self.rows // 8 + 1)]

            def write(e, at, new):
                for f in range(6):
                    dst[f, e, pl.ds(at, 8)] = new[f]

        else:
            tiles = [PAD + 8 * t for t in range(self.rows // 8)]

        many = next(n for n in PLANES if (stop - first) % n == 0)

        @pl.loop(0, (stop - first) // many)
        def _(i):
            for p in range(many):
                e = first + many * i + p
                for at in tiles:
                    write(e, at, self.advance(src, e, at))


def part_kernel(turn, place_of, sizes, begin, parts, has_seam, gives_seam, out_from, fresh, table, *refs):
    refs, (even, odd) = list(refs[:-2]), refs[-2:]
    place = place_of()
    run = Round(turn, place, sizes, table, even, odd)
    end = begin
    seam = refs.pop(0) if has_seam else None
    index = refs.pop(0) if fresh else None
    halo = refs.pop(0)
    for planes, halo_from in parts:
        run.fill(refs.pop(0), halo, planes, end, halo_from)
        end += planes
    next_seam = refs.pop() if gives_seam else None
    outs = [(ref, o + STEPS, o + STEPS + ref.shape[1]) for ref, o in zip(refs, out_from)]

    def bounds(step):
        return (begin if has_seam else 2 * step) - step, end - step

    def hold(level):
        if gives_seam:
            for plane in range(2):
                for f in range(6):
                    next_seam[level, f, plane] = run.levels[level][f, end - level - 2 + plane]

    def write(first, stop):
        targets = [(ref, at) for ref, at, until in outs if at <= first and stop <= until]

        def put(e, at, new):
            for ref, origin in targets:
                for i, f in enumerate(SENT):
                    ref[i, e - origin, pl.ds(at - PAD, 8)] = new[f]

        return put

    if has_seam:
        for level in range(STEPS):
            for plane in range(2):
                for f in range(6):
                    run.levels[level][f, begin - level - 2 + plane] = seam[level, f, plane]
    hold(0)
    for step in range(1, STEPS):
        run.sweep(step, *bounds(step))
        hold(step)
    marks = sorted(set(bounds(STEPS)) | set(m for _, *ends in outs for m in ends))
    for first, stop in zip(marks, marks[1:]):
        run.sweep(STEPS, first, stop, write(first, stop))

    if fresh:

        @pl.when(place == run.ng - 1)
        def _():
            for j in range(SHIFT):
                e = run.block - SHIFT + j + STEPS
                if any(at <= e < until for _, at, until in outs):
                    for t in range(run.rows // 8):
                        write(e, e + 1)(e, PAD + 8 * t, melt(table, index[turn, j, pl.ds(8 * t, 8)]))


def melt(table, row):
    mu = [jnp.zeros(row.shape, jnp.float32)] * 2
    for m in range((table.shape[0] - MELT) // 2):
        mu = [jnp.where(row == m, table[MELT + 2 * m + k], mu[k]) for k in range(2)]
    none = jnp.zeros(row.shape, jnp.float32)
    return [none, none, none, none + 1.0] + mu


def finish_kernel(place_of, ng, turn, table, index, *refs):
    pieces, (phases, potentials) = refs[:-2], refs[-2:]

    def put(o, here, new):
        for a in range(4):
            phases[a, o, here] = new[a]
        for k in range(2):
            potentials[k, o, here] = new[4 + k]

    at = 0
    for part in pieces:

        @pl.loop(0, part.shape[1])
        def _(i, part=part, at=at):
            new = [part[f, i] for f in range(len(SENT))]
            new.insert(3, 1.0 - new[0] - new[1] - new[2])
            put(i + at, slice(None), new)

        at += part.shape[1]

    @pl.when(place_of() == ng - 1)
    def _():
        for j in range(SHIFT):
            for t in range(index.shape[2] // 8):
                here = pl.ds(8 * t, 8)
                put(at - SHIFT + j, here, melt(table, index[turn, j, here]))


def prepare_kernel(labels_in, roughness_in, potential_in, *refs):
    outs, (first_rows, final_rows), (labels, roughness, potential, sems) = refs[:-6], refs[-6:-4], refs[-4:]
    rows = labels.shape[1]
    block = labels.shape[0]
    starts = (0, outs[0].shape[1], block - outs[2].shape[1])
    ranges = [(ref, at, at + ref.shape[1]) for ref, at in zip(outs, starts)]
    marks = sorted(set(m for _, *ends in ranges for m in ends))
    copies = []
    for n, (first, stop) in enumerate(zip(marks, marks[1:])):
        span = pl.ds(first, stop - first)
        pairs = [(labels_in.at[span], labels.at[span])]
        pairs += [(roughness_in.at[a, span], roughness.at[a, span]) for a in range(4)]
        pairs += [(potential_in.at[k, span], potential.at[k, span]) for k in range(2)]
        copies.append([pltpu.make_async_copy(*pair, sems.at[n, i]) for i, pair in enumerate(pairs)])
        for copy in copies[-1]:
            copy.start()
    for n, (first, stop) in enumerate(zip(marks, marks[1:])):
        targets = [(ref, at) for ref, at, until in ranges if at <= first and stop <= until]
        for copy in copies[n]:
            copy.wait()

        @pl.loop(first, stop)
        def _(o, targets=targets):
            kind = labels[o]
            rough = [roughness[a, o] for a in range(4)]
            inverse = 1.0 / (3.0 + rough[0] + rough[1] + rough[2] + rough[3])
            new = [(jnp.where(kind == a, 3.0, 0.0) + rough[a]) * inverse for a in range(3)]
            new += [potential[0, o], potential[1, o]]
            for f, value in enumerate(new):
                for ref, at in targets:
                    ref[f, o - at] = value
                first_rows[f, o] = value[:STEPS]
                final_rows[f, o] = value[rows - STEPS :]


def on_device(ng, nl, labels, roughness, potential, grad_coef, composition, latent, diffusivity, melt_table, melt_index):
    block, rows, lanes = labels.shape
    vmem = pl.BlockSpec(memory_space=pltpu.VMEM)
    smem = pl.BlockSpec(memory_space=pltpu.SMEM)
    f32 = jnp.float32
    kept = block - SHIFT + STEPS
    lows = block - kept
    highs = SHIFT + STEPS - lows
    height = kept + lows + highs
    table = scalar_table(grad_coef, composition, latent, diffusivity, melt_table)

    def home(g, l):
        return g * nl + l

    def away(g, l):
        return (g // 2 * 2 + (l % 2 ^ (l // 2 % 2))) * nl + l // 2 * 2 + g % 2

    def home_place():
        return lax.axis_index("grow")

    def away_place():
        return lax.axis_index("grow") // 2 * 2 + lax.axis_index("lat") % 2

    blocks = [(g, l) for g in range(ng) for l in range(nl)]

    def moved(array, before, after, climb):
        route = [(before(g + climb, l), after(g, l)) for g, l in blocks if g + climb < ng]
        return lax.ppermute(array, AXES, route)

    def edges(parts):
        first = jnp.concatenate([p[:, :, :STEPS] for p in parts], axis=1)
        final = jnp.concatenate([p[:, :, rows - STEPS :] for p in parts], axis=1)
        return first, final

    def beside(first, final, where):
        left = lax.ppermute(final, AXES, [(where(g, l), where(g, (l + 1) % nl)) for g, l in blocks])
        right = lax.ppermute(first, AXES, [(where(g, (l + 1) % nl), where(g, l)) for g, l in blocks])
        return left, right

    def piece(planes, width=rows):
        return jax.ShapeDtypeStruct((len(SENT), planes, width, lanes), f32)

    def cost(planes, moved_bytes):
        return pl.CostEstimate(flops=130 * 6 * planes * rows * lanes, bytes_accessed=moved_bytes, transcendentals=0)

    seam_shape = jax.ShapeDtypeStruct((STEPS, 6, 2, rows + 2 * PAD, lanes), f32)
    scratch = [pltpu.VMEM((6, height, rows + 2 * PAD, lanes), f32)] * 2

    def limit(size):
        return pltpu.CompilerParams(vmem_limit_bytes=size << 20)

    def part(turn, begin, planes, has_seam, gives_seam, sent, fresh, *args):
        size = sum(n for n, _ in planes)
        return pl.pallas_call(
            functools.partial(
                part_kernel,
                turn,
                away_place,
                (ng, block, rows),
                begin,
                planes,
                has_seam,
                gives_seam,
                [o for o, _ in sent],
                fresh,
            ),
            out_shape=[piece(n) for _, n in sent] + [seam_shape] * gives_seam,
            in_specs=[smem] + [vmem] * len(args),
            out_specs=[vmem] * (len(sent) + gives_seam),
            scratch_shapes=scratch,
            compiler_params=limit(24),
            cost_estimate=cost(4 * size, 4000000),
            name="part",
        )(table, *args)

    away_index = lax.ppermute(melt_index, AXES, [(away(ng - 1, l) // nl * nl + l, away(ng - 1, l)) for l in range(nl)])

    front, back, own, first_rows, final_rows = pl.pallas_call(
        prepare_kernel,
        out_shape=[piece(n) for n in (highs, lows, kept)] + [piece(block, STEPS)] * 2,
        in_specs=[pl.BlockSpec(memory_space=pltpu.HBM)] * 3,
        out_specs=[vmem] * 5,
        scratch_shapes=[
            pltpu.VMEM(labels.shape, jnp.int32),
            pltpu.VMEM(roughness.shape, f32),
            pltpu.VMEM(potential.shape, f32),
            pltpu.SemaphoreType.DMA((4, 7)),
        ],
        compiler_params=limit(58),
        name="prepare",
    )(labels, roughness, potential)

    def packed(left, right, first, stop):
        return jnp.concatenate([left[:, first:stop], right[:, first:stop]], axis=2)

    own_parts = [(kept, 0)]
    left, right = beside(first_rows, final_rows, home)
    own = [moved(own, home, away, 0)]
    own_halo = moved(packed(left, right, lows, block), home, away, 0)
    front = moved(front, home, away, 1)
    halo = moved(packed(left, right, 0, lows + highs), home, away, 1)
    back = moved(back, home, away, 1)
    early, seam = part(0, 0, own_parts, False, True, [(0, lows)], False, own_halo, *own)
    low = moved(early, away, away, 1)
    high, seam = part(0, kept, [(highs, 0)], True, True, [(lows, highs)], True, seam, away_index, halo, front)
    above = moved(high, away, away, 1)
    (rest,) = part(
        0, kept + highs, [(lows, highs)], True, False, [(lows + highs, lows)], True, seam, away_index, halo, back
    )

    own_parts = [(highs, 0), (lows, highs)]
    for turn in range(1, ROUNDS):
        last = turn == ROUNDS - 1
        left, right = beside(*edges([early, high, rest]), away)
        own, own_halo = [high, rest], packed(left, right, lows, block)
        if turn > 1:
            above = moved(high, away, away, 1)
        halo = moved(packed(left, right, 0, lows + highs), away, away, 1)
        early, seam = part(turn, 0, own_parts, False, True, [(0, lows)], False, own_halo, *own)
        sent = moved(early, away, home if last else away, 0 if last else 1)
        if last:
            break
        high, rest = part(
            turn,
            kept,
            [(lows, 0), (highs, lows)],
            True,
            False,
            [(lows, highs), (lows + highs, lows)],
            True,
            seam,
            away_index,
            halo,
            low,
            above,
        )
        low = sent

    cut = 2
    middle, seam = part(
        turn, kept, [(lows, 0), (cut, lows)], True, True, [(lows, lows + cut)], False, seam, halo, low, above[:, :cut]
    )
    middle = moved(middle, away, home, 0)
    (final,) = part(
        turn,
        kept + lows + cut,
        [(highs - cut, lows + cut)],
        True,
        False,
        [(2 * lows + cut, highs - cut)],
        False,
        seam,
        halo,
        above[:, cut:],
    )
    final = moved(final, away, home, 0)
    return pl.pallas_call(
        functools.partial(finish_kernel, home_place, ng, turn),
        out_shape=[jax.ShapeDtypeStruct((n, block, rows, lanes), f32) for n in (4, 2)],
        in_specs=[smem] + [vmem] * 4,
        out_specs=[vmem] * 2,
        compiler_params=limit(8),
        name="finish",
    )(table, melt_index, sent, middle, final)


def solution(mesh):
    ng, nl = mesh.shape["grow"], mesh.shape["lat"]
    placed = (
        P("grow", "lat", None),
        P(None, "grow", "lat", None),
        P(None, "grow", "lat", None),
        P(),
        P(),
        P(),
        P(),
        P(),
        P(None, None, "lat", None),
    )
    return jax.shard_map(
        functools.partial(on_device, ng, nl),
        mesh=mesh,
        in_specs=placed,
        out_specs=(P(None, "grow", "lat", None), P(None, "grow", "lat", None)),
        check_vma=False,
    )
```

```python
import functools

import jax
import jax.numpy as jnp
from jax import lax
from jax.experimental import pallas as pl
from jax.experimental.pallas import tpu as pltpu
from jax.sharding import PartitionSpec as P


STEPS = 4
ROUNDS = 4
SHIFT = 8
SENT = (0, 1, 2, 4, 5)
PAD = 8
DT = 0.04
PLANES = (4, 3, 2, 1)
AXES = ("grow", "lat")
GRAD, CENTER, COUPLE, LATENT, RELEASE, SPREAD, STAY, MELT = 0, 12, 16, 24, 28, 36, 38, 40


def scalar_table(grad_coef, composition, latent, diffusivity, melt_table):
    scaled = DT * grad_coef
    return jnp.concatenate(
        [
            scaled.reshape(-1),
            1.0 + DT - 2.0 * jnp.sum(scaled, axis=1),
            (DT * (composition - jnp.mean(composition, axis=0))).reshape(-1),
            DT * (latent - jnp.mean(latent)),
            (composition - composition[3]).reshape(-1),
            DT * diffusivity,
            1.0 - 6.0 * DT * diffusivity,
            melt_table.reshape(-1),
        ]
    )


class Round:
    def __init__(self, turn, place, sizes, table, even, odd):
        self.ng, self.block, self.rows = sizes
        self.table, self.levels = table, (even, odd, even, odd)
        self.start = place * self.block + SHIFT * (turn + 1) - STEPS
        self.lowest = SHIFT * turn - self.start
        self.top = self.ng * self.block + SHIFT * turn - 1 - self.start

    def fill(self, source, halo, planes, to, halo_from, source_from):
        level = self.levels[0]

        @pl.loop(0, planes)
        def _(i):
            body = [source[f, i + source_from] for f in range(len(SENT))]
            side = [halo[f, i + halo_from] for f in range(len(SENT))]
            body.insert(3, 1.0 - body[0] - body[1] - body[2])
            side.insert(3, 1.0 - side[0] - side[1] - side[2])
            for f in range(6):
                level[f, i + to, PAD : PAD + self.rows] = body[f]
                level[f, i + to, PAD - STEPS : PAD] = side[f][:STEPS]
                level[f, i + to, PAD + self.rows : PAD + self.rows + STEPS] = side[f][STEPS:]

    def advance(self, src, e, at):
        table, window = self.table, pl.ds(at, 8)
        up, down = jnp.minimum(e + 1, self.top), jnp.maximum(e - 1, self.lowest)
        total = float(self.ng * self.block)
        theta = ((e + self.start).astype(jnp.float32) - 0.5 * total) / total
        mid = [src[f, e, window] for f in range(6)]
        gsum = [src[f, up, window] + src[f, down, window] for f in range(6)]
        xsum = [src[f, e, pl.ds(at + 1, 8)] + src[f, e, pl.ds(at - 1, 8)] for f in range(6)]
        ysum = [pltpu.roll(v, 1, 1) + pltpu.roll(v, v.shape[1] - 1, 1) for v in mid]
        spread = [
            table[GRAD + 3 * a] * gsum[a]
            + table[GRAD + 3 * a + 1] * xsum[a]
            + table[GRAD + 3 * a + 2] * ysum[a]
            + table[CENTER + a] * mid[a]
            for a in range(4)
        ]
        mean = 0.25 * (spread[0] + spread[1] + spread[2] + spread[3]) - 0.25
        trial = [
            spread[a]
            - mean
            - table[COUPLE + 2 * a] * mid[4]
            - table[COUPLE + 2 * a + 1] * mid[5]
            - table[LATENT + a] * theta
            for a in range(3)
        ]
        trial.append(1.0 - trial[0] - trial[1] - trial[2])
        clipped = [jnp.clip(t, 0.0, 1.0) for t in trial]
        inverse = 1.0 / (clipped[0] + clipped[1] + clipped[2] + clipped[3])
        new = [c * inverse for c in clipped]
        change = [n - v for n, v in zip(new[:3], mid[:3])]
        for k in range(2):
            release = table[RELEASE + k] * change[0]
            for a in range(1, 3):
                release = release + table[RELEASE + 2 * a + k] * change[a]
            sides = gsum[4 + k] + xsum[4 + k] + ysum[4 + k]
            new.append(table[SPREAD + k] * sides + table[STAY + k] * mid[4 + k] - release)
        return new

    def sweep(self, step, first, stop, write=None):
        src, dst = self.levels[step - 1], self.levels[step % STEPS]
        if write is None:
            tiles = [PAD - STEPS + 8 * t for t in range(self.rows // 8 + 1)]

            def write(e, at, new):
                for f in range(6):
                    dst[f, e, pl.ds(at, 8)] = new[f]

        else:
            tiles = [PAD + 8 * t for t in range(self.rows // 8)]

        many = next(n for n in PLANES if (stop - first) % n == 0)

        @pl.loop(0, (stop - first) // many)
        def _(i):
            for p in range(many):
                e = first + many * i + p
                for at in tiles:
                    write(e, at, self.advance(src, e, at))


def part_kernel(turn, place_of, sizes, begin, parts, has_seam, gives_seam, out_from, fresh, table, *refs):
    refs, (even, odd) = list(refs[:-2]), refs[-2:]
    place = place_of()
    run = Round(turn, place, sizes, table, even, odd)
    end = begin
    seam = refs.pop(0) if has_seam else None
    index = refs.pop(0) if fresh else None
    halo = refs.pop(0)
    for planes, halo_from, source_from in parts:
        run.fill(refs.pop(0), halo, planes, end, halo_from, source_from)
        end += planes
    next_seam = refs.pop() if gives_seam else None
    outs = [(ref, o + STEPS, o + STEPS + ref.shape[1]) for ref, o in zip(refs, out_from)]

    def bounds(step):
        return (begin if has_seam else 2 * step) - step, end - step

    def hold(level):
        if gives_seam:
            for plane in range(2):
                for f in range(6):
                    next_seam[level, f, plane] = run.levels[level][f, end - level - 2 + plane]

    def write(first, stop):
        targets = [(ref, at) for ref, at, until in outs if at <= first and stop <= until]

        def put(e, at, new):
            for ref, origin in targets:
                for i, f in enumerate(SENT):
                    ref[i, e - origin, pl.ds(at - PAD, 8)] = new[f]

        return put

    if has_seam:
        for level in range(STEPS):
            for plane in range(2):
                for f in range(6):
                    run.levels[level][f, begin - level - 2 + plane] = seam[level, f, plane]
    hold(0)
    for step in range(1, STEPS):
        run.sweep(step, *bounds(step))
        hold(step)
    marks = sorted(set(bounds(STEPS)) | set(m for _, *ends in outs for m in ends))
    for first, stop in zip(marks, marks[1:]):
        run.sweep(STEPS, first, stop, write(first, stop))

    if fresh:

        @pl.when(place == run.ng - 1)
        def _():
            for j in range(SHIFT):
                e = run.block - SHIFT + j + STEPS
                if any(at <= e < until for _, at, until in outs):
                    for t in range(run.rows // 8):
                        write(e, e + 1)(e, PAD + 8 * t, melt(table, index[turn, j, pl.ds(8 * t, 8)]))


def melt(table, row):
    mu = [jnp.zeros(row.shape, jnp.float32)] * 2
    for m in range((table.shape[0] - MELT) // 2):
        mu = [jnp.where(row == m, table[MELT + 2 * m + k], mu[k]) for k in range(2)]
    none = jnp.zeros(row.shape, jnp.float32)
    return [none, none, none, none + 1.0] + mu


def finish_kernel(place_of, ng, turn, table, index, *refs):
    pieces, (phases, potentials) = refs[:-2], refs[-2:]

    def put(o, here, new):
        for a in range(4):
            phases[a, o, here] = new[a]
        for k in range(2):
            potentials[k, o, here] = new[4 + k]

    at = 0
    for part in pieces:

        @pl.loop(0, part.shape[1])
        def _(i, part=part, at=at):
            new = [part[f, i] for f in range(len(SENT))]
            new.insert(3, 1.0 - new[0] - new[1] - new[2])
            put(i + at, slice(None), new)

        at += part.shape[1]

    @pl.when(place_of() == ng - 1)
    def _():
        for j in range(SHIFT):
            for t in range(index.shape[2] // 8):
                here = pl.ds(8 * t, 8)
                put(at - SHIFT + j, here, melt(table, index[turn, j, here]))


def prepare_kernel(labels_in, roughness_in, potential_in, *refs):
    outs, (first_rows, final_rows), (labels, roughness, potential, sems) = refs[:-6], refs[-6:-4], refs[-4:]
    rows = labels.shape[1]
    starts = (0, outs[0].shape[1])
    ranges = [(ref, at, at + ref.shape[1]) for ref, at in zip(outs, starts)]
    marks = sorted(set(m for _, *ends in ranges for m in ends))
    copies = []
    for n, (first, stop) in enumerate(zip(marks, marks[1:])):
        span = pl.ds(first, stop - first)
        pairs = [(labels_in.at[span], labels.at[span])]
        pairs += [(roughness_in.at[a, span], roughness.at[a, span]) for a in range(4)]
        pairs += [(potential_in.at[k, span], potential.at[k, span]) for k in range(2)]
        copies.append([pltpu.make_async_copy(*pair, sems.at[n, i]) for i, pair in enumerate(pairs)])
        for copy in copies[-1]:
            copy.start()
    for n, (first, stop) in enumerate(zip(marks, marks[1:])):
        targets = [(ref, at) for ref, at, until in ranges if at <= first and stop <= until]
        for copy in copies[n]:
            copy.wait()

        @pl.loop(first, stop)
        def _(o, targets=targets):
            kind = labels[o]
            rough = [roughness[a, o] for a in range(4)]
            inverse = 1.0 / (3.0 + rough[0] + rough[1] + rough[2] + rough[3])
            new = [(jnp.where(kind == a, 3.0, 0.0) + rough[a]) * inverse for a in range(3)]
            new += [potential[0, o], potential[1, o]]
            for f, value in enumerate(new):
                for ref, at in targets:
                    ref[f, o - at] = value
                first_rows[f, o] = value[:STEPS]
                final_rows[f, o] = value[rows - STEPS :]


def on_device(ng, nl, labels, roughness, potential, grad_coef, composition, latent, diffusivity, melt_table, melt_index):
    block, rows, lanes = labels.shape
    vmem = pl.BlockSpec(memory_space=pltpu.VMEM)
    smem = pl.BlockSpec(memory_space=pltpu.SMEM)
    f32 = jnp.float32
    kept = block - SHIFT + STEPS
    lows = block - kept
    highs = SHIFT + STEPS - lows
    height = kept + lows + highs
    table = scalar_table(grad_coef, composition, latent, diffusivity, melt_table)

    def home(g, l):
        return g * nl + l

    def away(g, l):
        return (g // 2 * 2 + (l % 2 ^ (l // 2 % 2))) * nl + l // 2 * 2 + g % 2

    def home_place():
        return lax.axis_index("grow")

    def away_place():
        return lax.axis_index("grow") // 2 * 2 + lax.axis_index("lat") % 2

    blocks = [(g, l) for g in range(ng) for l in range(nl)]

    def moved(array, before, after, climb):
        route = [(before(g + climb, l), after(g, l)) for g, l in blocks if g + climb < ng]
        return lax.ppermute(array, AXES, route)

    def edges(parts):
        first = jnp.concatenate([p[:, :, :STEPS] for p in parts], axis=1)
        final = jnp.concatenate([p[:, :, rows - STEPS :] for p in parts], axis=1)
        return first, final

    def beside(first, final, where):
        left = lax.ppermute(final, AXES, [(where(g, l), where(g, (l + 1) % nl)) for g, l in blocks])
        right = lax.ppermute(first, AXES, [(where(g, (l + 1) % nl), where(g, l)) for g, l in blocks])
        return left, right

    def piece(planes, width=rows):
        return jax.ShapeDtypeStruct((len(SENT), planes, width, lanes), f32)

    def cost(planes, moved_bytes):
        return pl.CostEstimate(flops=130 * 6 * planes * rows * lanes, bytes_accessed=moved_bytes, transcendentals=0)

    seam_shape = jax.ShapeDtypeStruct((STEPS, 6, 2, rows + 2 * PAD, lanes), f32)
    scratch = [pltpu.VMEM((6, height, rows + 2 * PAD, lanes), f32)] * 2

    def limit(size):
        return pltpu.CompilerParams(vmem_limit_bytes=size << 20)

    def part(turn, begin, planes, has_seam, gives_seam, sent, fresh, *args):
        size = sum(n for n, _, _ in planes)
        return pl.pallas_call(
            functools.partial(
                part_kernel,
                turn,
                away_place,
                (ng, block, rows),
                begin,
                planes,
                has_seam,
                gives_seam,
                [o for o, _ in sent],
                fresh,
            ),
            out_shape=[piece(n) for _, n in sent] + [seam_shape] * gives_seam,
            in_specs=[smem] + [vmem] * len(args),
            out_specs=[vmem] * (len(sent) + gives_seam),
            scratch_shapes=scratch,
            compiler_params=limit(24),
            cost_estimate=cost(4 * size, 4000000),
            name="part",
        )(table, *args)

    away_index = lax.ppermute(
        melt_index, AXES, [(away(ng - 1, l) // nl * nl + l, away(ng - 1, l)) for l in range(nl)]
    )

    front, back, first_rows, final_rows = pl.pallas_call(
        prepare_kernel,
        out_shape=[piece(highs), piece(block - highs)] + [piece(block, STEPS)] * 2,
        in_specs=[pl.BlockSpec(memory_space=pltpu.HBM)] * 3,
        out_specs=[vmem] * 4,
        scratch_shapes=[
            pltpu.VMEM(labels.shape, jnp.int32),
            pltpu.VMEM(roughness.shape, f32),
            pltpu.VMEM(potential.shape, f32),
            pltpu.SemaphoreType.DMA((2, 7)),
        ],
        compiler_params=limit(58),
        name="prepare",
    )(labels, roughness, potential)

    def packed(left, right, first, stop):
        return jnp.concatenate([left[:, first:stop], right[:, first:stop]], axis=2)

    front = moved(front, home, away, 0)
    left, right = beside(first_rows, final_rows, home)
    back = moved(back, home, away, 0)
    sides = moved(packed(left, right, 0, block), home, away, 0)
    above = moved(front, away, away, 1)
    above2 = moved(back[:, :lows], away, away, 1)
    halo = moved(sides, away, away, 1)
    early, seam = part(
        0,
        0,
        [(highs - lows, lows, lows), (block - highs, highs, 0)],
        False,
        True,
        [(0, lows)],
        False,
        sides,
        front,
        back,
    )
    low = moved(early, away, away, 1)
    high, rest = part(
        0,
        kept,
        [(highs, 0, 0), (lows, highs, 0)],
        True,
        False,
        [(lows, highs), (lows + highs, lows)],
        True,
        seam,
        away_index,
        halo,
        above,
        above2,
    )

    own_parts = [(highs, 0, 0), (lows, highs, 0)]
    for turn in range(1, ROUNDS):
        last = turn == ROUNDS - 1
        left, right = beside(*edges([early, high, rest]), away)
        own, own_halo = [high, rest], packed(left, right, lows, block)
        above = moved(high, away, away, 1)
        halo = moved(packed(left, right, 0, lows + highs), away, away, 1)
        early, seam = part(turn, 0, own_parts, False, True, [(0, lows)], False, own_halo, *own)
        sent = moved(early, away, home if last else away, 0 if last else 1)
        if last:
            break
        high, rest = part(
            turn,
            kept,
            [(lows, 0, 0), (highs, lows, 0)],
            True,
            False,
            [(lows, highs), (lows + highs, lows)],
            True,
            seam,
            away_index,
            halo,
            low,
            above,
        )
        low = sent

    cut = 2
    middle, seam = part(
        turn,
        kept,
        [(lows, 0, 0), (cut, lows, 0)],
        True,
        True,
        [(lows, lows + cut)],
        False,
        seam,
        halo,
        low,
        above,
    )
    middle = moved(middle, away, home, 0)
    (final,) = part(
        turn,
        kept + lows + cut,
        [(highs - cut, lows + cut, cut)],
        True,
        False,
        [(2 * lows + cut, highs - cut)],
        False,
        seam,
        halo,
        above,
    )
    final = moved(final, away, home, 0)
    return pl.pallas_call(
        functools.partial(finish_kernel, home_place, ng, turn),
        out_shape=[jax.ShapeDtypeStruct((n, block, rows, lanes), f32) for n in (4, 2)],
        in_specs=[smem] + [vmem] * 4,
        out_specs=[vmem] * 2,
        compiler_params=limit(8),
        name="finish",
    )(table, melt_index, sent, middle, final)


def solution(mesh):
    ng, nl = mesh.shape["grow"], mesh.shape["lat"]
    placed = (
        P("grow", "lat", None),
        P(None, "grow", "lat", None),
        P(None, "grow", "lat", None),
        P(),
        P(),
        P(),
        P(),
        P(),
        P(None, None, "lat", None),
    )
    return jax.shard_map(
        functools.partial(on_device, ng, nl),
        mesh=mesh,
        in_specs=placed,
        out_specs=(P(None, "grow", "lat", None), P(None, "grow", "lat", None)),
        check_vma=False,
    )
```

```python
import functools

import jax
import jax.numpy as jnp
from jax import lax
from jax.experimental import pallas as pl
from jax.experimental.pallas import tpu as pltpu
from jax.sharding import PartitionSpec as P


STEPS = 4
ROUNDS = 4
SHIFT = 8
SENT = (0, 1, 2, 4, 5)
PAD = 8
DT = 0.04
PLANES = (4, 3, 2, 1)
AXES = ("grow", "lat")
GRAD, CENTER, COUPLE, LATENT, RELEASE, SPREAD, STAY, MELT = 0, 12, 16, 24, 28, 36, 38, 40


def scalar_table(grad_coef, composition, latent, diffusivity, melt_table):
    scaled = DT * grad_coef
    return jnp.concatenate(
        [
            scaled.reshape(-1),
            1.0 + DT - 2.0 * jnp.sum(scaled, axis=1),
            (DT * (composition - jnp.mean(composition, axis=0))).reshape(-1),
            DT * (latent - jnp.mean(latent)),
            (composition - composition[3]).reshape(-1),
            DT * diffusivity,
            1.0 - 6.0 * DT * diffusivity,
            melt_table.reshape(-1),
        ]
    )


class Round:
    def __init__(self, turn, place, sizes, table, even, odd):
        self.ng, self.block, self.rows = sizes
        self.table, self.levels = table, (even, odd, even, odd)
        self.start = place * self.block + SHIFT * (turn + 1) - STEPS
        self.lowest = SHIFT * turn - self.start
        self.top = self.ng * self.block + SHIFT * turn - 1 - self.start

    def fill(self, source, halo, planes, to, halo_from, source_from):
        level = self.levels[0]

        @pl.loop(0, planes)
        def _(i):
            body = [source[f, i + source_from] for f in range(len(SENT))]
            side = [halo[f, i + halo_from] for f in range(len(SENT))]
            body.insert(3, 1.0 - body[0] - body[1] - body[2])
            side.insert(3, 1.0 - side[0] - side[1] - side[2])
            for f in range(6):
                level[f, i + to, PAD : PAD + self.rows] = body[f]
                level[f, i + to, PAD - STEPS : PAD] = side[f][:STEPS]
                level[f, i + to, PAD + self.rows : PAD + self.rows + STEPS] = side[f][STEPS:]

    def advance(self, src, e, at):
        table, window = self.table, pl.ds(at, 8)
        up, down = jnp.minimum(e + 1, self.top), jnp.maximum(e - 1, self.lowest)
        total = float(self.ng * self.block)
        theta = ((e + self.start).astype(jnp.float32) - 0.5 * total) / total
        mid = [src[f, e, window] for f in range(6)]
        gsum = [src[f, up, window] + src[f, down, window] for f in range(6)]
        xsum = [src[f, e, pl.ds(at + 1, 8)] + src[f, e, pl.ds(at - 1, 8)] for f in range(6)]
        ysum = [pltpu.roll(v, 1, 1) + pltpu.roll(v, v.shape[1] - 1, 1) for v in mid]
        spread = [
            table[GRAD + 3 * a] * gsum[a]
            + table[GRAD + 3 * a + 1] * xsum[a]
            + table[GRAD + 3 * a + 2] * ysum[a]
            + table[CENTER + a] * mid[a]
            for a in range(4)
        ]
        mean = 0.25 * (spread[0] + spread[1] + spread[2] + spread[3]) - 0.25
        trial = [
            spread[a]
            - mean
            - table[COUPLE + 2 * a] * mid[4]
            - table[COUPLE + 2 * a + 1] * mid[5]
            - table[LATENT + a] * theta
            for a in range(3)
        ]
        trial.append(1.0 - trial[0] - trial[1] - trial[2])
        clipped = [jnp.clip(t, 0.0, 1.0) for t in trial]
        inverse = 1.0 / (clipped[0] + clipped[1] + clipped[2] + clipped[3])
        new = [c * inverse for c in clipped]
        change = [n - v for n, v in zip(new[:3], mid[:3])]
        for k in range(2):
            release = table[RELEASE + k] * change[0]
            for a in range(1, 3):
                release = release + table[RELEASE + 2 * a + k] * change[a]
            sides = gsum[4 + k] + xsum[4 + k] + ysum[4 + k]
            new.append(table[SPREAD + k] * sides + table[STAY + k] * mid[4 + k] - release)
        return new

    def sweep(self, step, first, stop, write=None):
        src, dst = self.levels[step - 1], self.levels[step % STEPS]
        if write is None:
            tiles = [PAD - STEPS + 8 * t for t in range(self.rows // 8 + 1)]

            def write(e, at, new):
                for f in range(6):
                    dst[f, e, pl.ds(at, 8)] = new[f]

        else:
            tiles = [PAD + 8 * t for t in range(self.rows // 8)]

        many = next(n for n in PLANES if (stop - first) % n == 0)

        @pl.loop(0, (stop - first) // many)
        def _(i):
            for p in range(many):
                e = first + many * i + p
                for at in tiles:
                    write(e, at, self.advance(src, e, at))


def part_kernel(turn, place_of, sizes, begin, parts, has_seam, gives_seam, out_from, fresh, table, *refs):
    refs, (even, odd) = list(refs[:-2]), refs[-2:]
    place = place_of()
    run = Round(turn, place, sizes, table, even, odd)
    end = begin
    seam = refs.pop(0) if has_seam else None
    index = refs.pop(0) if fresh else None
    halo = refs.pop(0)
    for planes, halo_from, source_from in parts:
        run.fill(refs.pop(0), halo, planes, end, halo_from, source_from)
        end += planes
    next_seam = refs.pop() if gives_seam else None
    outs = [(ref, o + STEPS, o + STEPS + ref.shape[1]) for ref, o in zip(refs, out_from)]

    def bounds(step):
        return (begin if has_seam else 2 * step) - step, end - step

    def hold(level):
        if gives_seam:
            for plane in range(2):
                for f in range(6):
                    next_seam[level, f, plane] = run.levels[level][f, end - level - 2 + plane]

    def write(first, stop):
        targets = [(ref, at) for ref, at, until in outs if at <= first and stop <= until]

        def put(e, at, new):
            for ref, origin in targets:
                for i, f in enumerate(SENT):
                    ref[i, e - origin, pl.ds(at - PAD, 8)] = new[f]

        return put

    if has_seam:
        for level in range(STEPS):
            for plane in range(2):
                for f in range(6):
                    run.levels[level][f, begin - level - 2 + plane] = seam[level, f, plane]
    hold(0)
    for step in range(1, STEPS):
        run.sweep(step, *bounds(step))
        hold(step)
    marks = sorted(set(bounds(STEPS)) | set(m for _, *ends in outs for m in ends))
    for first, stop in zip(marks, marks[1:]):
        run.sweep(STEPS, first, stop, write(first, stop))

    if fresh:

        @pl.when(place == run.ng - 1)
        def _():
            for j in range(SHIFT):
                e = run.block - SHIFT + j + STEPS
                if any(at <= e < until for _, at, until in outs):
                    for t in range(run.rows // 8):
                        write(e, e + 1)(e, PAD + 8 * t, melt(table, index[turn, j, pl.ds(8 * t, 8)]))


def melt(table, row):
    mu = [jnp.zeros(row.shape, jnp.float32)] * 2
    for m in range((table.shape[0] - MELT) // 2):
        mu = [jnp.where(row == m, table[MELT + 2 * m + k], mu[k]) for k in range(2)]
    none = jnp.zeros(row.shape, jnp.float32)
    return [none, none, none, none + 1.0] + mu


def finish_kernel(place_of, ng, turn, table, index, *refs):
    pieces, (phases, potentials) = refs[:-2], refs[-2:]

    def put(o, here, new):
        for a in range(4):
            phases[a, o, here] = new[a]
        for k in range(2):
            potentials[k, o, here] = new[4 + k]

    at = 0
    for part in pieces:

        @pl.loop(0, part.shape[1])
        def _(i, part=part, at=at):
            new = [part[f, i] for f in range(len(SENT))]
            new.insert(3, 1.0 - new[0] - new[1] - new[2])
            put(i + at, slice(None), new)

        at += part.shape[1]

    @pl.when(place_of() == ng - 1)
    def _():
        for j in range(SHIFT):
            for t in range(index.shape[2] // 8):
                here = pl.ds(8 * t, 8)
                put(at - SHIFT + j, here, melt(table, index[turn, j, here]))


def prepare_kernel(first, labels_in, roughness_in, potential_in, *refs):
    before, (state, first_rows, final_rows), (labels, roughness, potential, sems) = refs[:-7], refs[-7:-4], refs[-4:]
    planes, rows = labels.shape[:2]
    span = pl.ds(first, planes)
    pairs = [(labels_in.at[span], labels)]
    pairs += [(roughness_in.at[a, span], roughness.at[a]) for a in range(4)]
    pairs += [(potential_in.at[k, span], potential.at[k]) for k in range(2)]
    copies = [pltpu.make_async_copy(*pair, sems.at[i]) for i, pair in enumerate(pairs)]
    for copy in copies:
        copy.start()
    for old, new in zip(before, (first_rows, final_rows)):
        new[:, :first] = old[...]
    for copy in copies:
        copy.wait()

    @pl.loop(0, planes)
    def _(o):
        kind = labels[o]
        rough = [roughness[a, o] for a in range(4)]
        inverse = 1.0 / (3.0 + rough[0] + rough[1] + rough[2] + rough[3])
        new = [(jnp.where(kind == a, 3.0, 0.0) + rough[a]) * inverse for a in range(3)]
        new += [potential[0, o], potential[1, o]]
        for f, value in enumerate(new):
            state[f, o] = value
            first_rows[f, o + first] = value[:STEPS]
            final_rows[f, o + first] = value[rows - STEPS :]


def on_device(ng, nl, labels, roughness, potential, grad_coef, composition, latent, diffusivity, melt_table, melt_index):
    block, rows, lanes = labels.shape
    vmem = pl.BlockSpec(memory_space=pltpu.VMEM)
    smem = pl.BlockSpec(memory_space=pltpu.SMEM)
    f32 = jnp.float32
    kept = block - SHIFT + STEPS
    lows = block - kept
    highs = SHIFT + STEPS - lows
    height = kept + lows + highs
    table = scalar_table(grad_coef, composition, latent, diffusivity, melt_table)

    def home(g, l):
        return g * nl + l

    def away(g, l):
        return (g // 2 * 2 + (l % 2 ^ (l // 2 % 2))) * nl + l // 2 * 2 + g % 2

    def home_place():
        return lax.axis_index("grow")

    def away_place():
        return lax.axis_index("grow") // 2 * 2 + lax.axis_index("lat") % 2

    blocks = [(g, l) for g in range(ng) for l in range(nl)]

    def moved(array, before, after, climb):
        route = [(before(g + climb, l), after(g, l)) for g, l in blocks if g + climb < ng]
        return lax.ppermute(array, AXES, route)

    def edges(parts):
        first = jnp.concatenate([p[:, :, :STEPS] for p in parts], axis=1)
        final = jnp.concatenate([p[:, :, rows - STEPS :] for p in parts], axis=1)
        return first, final

    def beside(first, final, where):
        left = lax.ppermute(final, AXES, [(where(g, l), where(g, (l + 1) % nl)) for g, l in blocks])
        right = lax.ppermute(first, AXES, [(where(g, (l + 1) % nl), where(g, l)) for g, l in blocks])
        return left, right

    def piece(planes, width=rows):
        return jax.ShapeDtypeStruct((len(SENT), planes, width, lanes), f32)

    def cost(planes, moved_bytes):
        return pl.CostEstimate(flops=130 * 6 * planes * rows * lanes, bytes_accessed=moved_bytes, transcendentals=0)

    seam_shape = jax.ShapeDtypeStruct((STEPS, 6, 2, rows + 2 * PAD, lanes), f32)
    scratch = [pltpu.VMEM((6, height, rows + 2 * PAD, lanes), f32)] * 2

    def limit(size):
        return pltpu.CompilerParams(vmem_limit_bytes=size << 20)

    def part(turn, begin, planes, has_seam, gives_seam, sent, fresh, *args):
        size = sum(n for n, _, _ in planes)
        return pl.pallas_call(
            functools.partial(
                part_kernel,
                turn,
                away_place,
                (ng, block, rows),
                begin,
                planes,
                has_seam,
                gives_seam,
                [o for o, _ in sent],
                fresh,
            ),
            out_shape=[piece(n) for _, n in sent] + [seam_shape] * gives_seam,
            in_specs=[smem] + [vmem] * len(args),
            out_specs=[vmem] * (len(sent) + gives_seam),
            scratch_shapes=scratch,
            compiler_params=limit(24),
            cost_estimate=cost(4 * size, 4000000),
            name="part",
        )(table, *args)

    away_index = lax.ppermute(melt_index, AXES, [(away(ng - 1, l) // nl * nl + l, away(ng - 1, l)) for l in range(nl)])

    def prepare(first, planes, *before):
        return pl.pallas_call(
            functools.partial(prepare_kernel, first),
            out_shape=[piece(planes)] + [piece(first + planes, STEPS)] * 2,
            in_specs=[pl.BlockSpec(memory_space=pltpu.HBM)] * 3 + [vmem] * len(before),
            out_specs=[vmem] * 3,
            scratch_shapes=[
                pltpu.VMEM((planes, rows, lanes), jnp.int32),
                pltpu.VMEM((4, planes, rows, lanes), f32),
                pltpu.VMEM((2, planes, rows, lanes), f32),
                pltpu.SemaphoreType.DMA((7,)),
            ],
            compiler_params=limit(58),
            name="prepare",
        )(labels, roughness, potential, *before)

    front, *edge_rows = prepare(0, highs)
    back, first_rows, final_rows = prepare(highs, block - highs, *edge_rows)

    def packed(left, right, first, stop):
        return jnp.concatenate([left[:, first:stop], right[:, first:stop]], axis=2)

    front = moved(front, home, away, 0)
    left, right = beside(first_rows, final_rows, home)
    back = moved(back, home, away, 0)
    sides = moved(packed(left, right, 0, block), home, away, 0)
    above = moved(front, away, away, 1)
    above2 = moved(back[:, :lows], away, away, 1)
    halo = moved(sides, away, away, 1)
    early, seam = part(
        0,
        0,
        [(highs - lows, lows, lows), (block - highs, highs, 0)],
        False,
        True,
        [(0, lows)],
        False,
        sides,
        front,
        back,
    )
    low = moved(early, away, away, 1)
    high, rest = part(
        0,
        kept,
        [(highs, 0, 0), (lows, highs, 0)],
        True,
        False,
        [(lows, highs), (lows + highs, lows)],
        True,
        seam,
        away_index,
        halo,
        above,
        above2,
    )

    own_parts = [(highs, 0, 0), (lows, highs, 0)]
    for turn in range(1, ROUNDS):
        last = turn == ROUNDS - 1
        left, right = beside(*edges([early, high, rest]), away)
        own, own_halo = [high, rest], packed(left, right, lows, block)
        above = moved(high, away, away, 1)
        halo = moved(packed(left, right, 0, lows + highs), away, away, 1)
        early, seam = part(turn, 0, own_parts, False, True, [(0, lows)], False, own_halo, *own)
        sent = moved(early, away, home if last else away, 0 if last else 1)
        if last:
            break
        high, rest = part(
            turn,
            kept,
            [(lows, 0, 0), (highs, lows, 0)],
            True,
            False,
            [(lows, highs), (lows + highs, lows)],
            True,
            seam,
            away_index,
            halo,
            low,
            above,
        )
        low = sent

    cut = 2
    middle, seam = part(
        turn, kept, [(lows, 0, 0), (cut, lows, 0)], True, True, [(lows, lows + cut)], False, seam, halo, low, above
    )
    middle = moved(middle, away, home, 0)
    (final,) = part(
        turn,
        kept + lows + cut,
        [(highs - cut, lows + cut, cut)],
        True,
        False,
        [(2 * lows + cut, highs - cut)],
        False,
        seam,
        halo,
        above,
    )
    final = moved(final, away, home, 0)
    return pl.pallas_call(
        functools.partial(finish_kernel, home_place, ng, turn),
        out_shape=[jax.ShapeDtypeStruct((n, block, rows, lanes), f32) for n in (4, 2)],
        in_specs=[smem] + [vmem] * 4,
        out_specs=[vmem] * 2,
        compiler_params=limit(8),
        name="finish",
    )(table, melt_index, sent, middle, final)


def solution(mesh):
    ng, nl = mesh.shape["grow"], mesh.shape["lat"]
    placed = (
        P("grow", "lat", None),
        P(None, "grow", "lat", None),
        P(None, "grow", "lat", None),
        P(),
        P(),
        P(),
        P(),
        P(),
        P(None, None, "lat", None),
    )
    return jax.shard_map(
        functools.partial(on_device, ng, nl),
        mesh=mesh,
        in_specs=placed,
        out_specs=(P(None, "grow", "lat", None), P(None, "grow", "lat", None)),
        check_vma=False,
    )
```
